128 devices in a mesh: dp: 64 (over y_lo, z, x, core), feat: 2 (over y_hi).
Axes of the slice: x: 4, y: 4 (y_hi: 2, y_lo: 2; y = y_hi * 2 + y_lo), z: 4, core: 2. Of those that a mesh axis runs over, the one named last changes fastest.
Arguments:
- grads: bfloat16 [32768, 4096], P('dp', 'feat'), may hold values from -16 to 16
- covariance: float32 [4096, 4096], P('dp', 'feat'), may hold values from -0.16 to 6, as said below
- test_grads: bfloat16 [512, 4096], P('feat', 'dp'), may hold values from -0.09375 to 0.09375
- inverse_factor: bfloat16 [4096, 4096], P('dp'), may hold values from -0.09375 to 0.09375
Outputs:
- scores: float32 [32768, 512], P('dp', 'feat')
- covariance_out: float32 [4096, 4096], P('dp', 'feat')
The draws below stay inside these ranges and needn't reach their ends.
Inputs may be any that keep to these rules, and one draw needn't show every extreme that they name: covariance is symmetric.
All inputs are finite; a program needn't handle non-finite values.
Results may differ from the reference program's by a relative error of at most 0.0029.
Values may be sent and summed in bfloat16 or wider, within the bound.
No kernel may reach another device: no remote copies, remote signals or barrier semaphores. Data moves between devices by JAX's collectives and lax.ppermute only.
A program may use at most 192 MiB of HBM per device.

```python
import jax
import jax.numpy as jnp

K = 4096
M = 512
TOKENS = 32768


def draw_covariance(key, part):
    base_key = jax.random.fold_in(key, 11)
    noise_key, diag_key = jax.random.split(base_key, 2)
    noise = jnp.clip(jax.random.normal(noise_key, (K, K), jnp.float32) * 0.007, -0.04, 0.04)
    symmetric = (noise + noise.T) * 0.5
    identity_mat = jnp.eye(K, dtype=jnp.float32)
    diagonal = jax.random.uniform(diag_key, (K,), jnp.float32, 0.5, 1.5)
    result = symmetric * (1.0 - identity_mat) + identity_mat * diagonal[None, :]
    return result


def strengthened(drawn, own_key, source, target, blocks, factor):
    owner, partner = [(jnp.arange(drawn.shape[dim]) // (drawn.shape[dim] // blocks)).reshape([-1 if axis == dim else 1 for axis in range(drawn.ndim)]) for dim in (source, target)]
    chosen = jax.random.permutation(own_key, blocks)[partner]
    strong = (owner == chosen) | (owner == (partner + blocks // 2) % blocks)
    return jnp.where(strong, factor * drawn, drawn)


def shard_levels(key, dims, shards, low, largest):
    gain = 1.0
    for dim, parts in shards:
        steps = jax.random.uniform(jax.random.fold_in(jax.random.fold_in(key, 6), dim), (parts,), jnp.float32, low / len(shards), largest / len(shards))
        gain = gain * jnp.repeat(jnp.exp(steps), dims[dim] // parts).reshape((-1,) + (1,) * (len(dims) - 1 - dim))
    return gain


def scatter_about(own_key, dims, deviation, bound, shards=(), kind=jnp.bfloat16):
    values = deviation * jax.random.normal(own_key, dims, jnp.float32)
    if shards:
        values = values * shard_levels(own_key, dims, shards, -0.22, 0.18)
    return jnp.clip(values, -bound, bound).astype(kind)


def gaussian_with(stream_key, shape, spread, most, cuts, heavy, held_as=jnp.bfloat16):
    drawn = spread * jax.random.normal(stream_key, shape, jnp.float32)
    if cuts:
        drawn = drawn * shard_levels(stream_key, shape, cuts, -0.22, 0.18)
    return jnp.clip(strengthened(drawn, jax.random.fold_in(stream_key, 3), *heavy), -most, most).astype(held_as)


def setup_inputs(seed: int = 0) -> dict:
    seeds = jax.random.split(jax.random.key(seed), 5)
    grads = gaussian_with(seeds[0], (TOKENS, K), 1.0, 16.0, ((0, 64), (1, 2)), (0, 1, 64, 4.0))
    covariance = draw_covariance(jax.random.fold_in(seeds[4], 71), 0)
    test_grads = scatter_about(seeds[2], (M, K), K ** -0.5, 0.09375, ((0, 2), (1, 64)))
    inverse_factor = scatter_about(seeds[3], (K, K), K ** -0.5, 0.09375, ((0, 64),))
    return {"grads": grads, "covariance": covariance, "test_grads": test_grads, "inverse_factor": inverse_factor}


def reference(grads, covariance, test_grads, inverse_factor):
    term = jnp.dot(grads.T, grads, preferred_element_type=jnp.float32)
    covariance_out = 0.9 * covariance + term / TOKENS
    preconditioned = jnp.dot(test_grads, inverse_factor, preferred_element_type=jnp.float32).astype(jnp.bfloat16)
    scores = jnp.dot(grads, preconditioned.T, preferred_element_type=jnp.float32)
    return scores, covariance_out
```

```python
import functools

import jax
import jax.numpy as jnp
import numpy as np
from jax import lax
from jax.experimental import pallas as pl
from jax.experimental.pallas import tpu as pltpu
from jax.sharding import Mesh
from jax.sharding import PartitionSpec as P

AXES = ("yl", "z", "x", "c", "yh")
SIZES = (2, 4, 4, 2, 2)
DP = ("yl", "z", "x", "c")
bf16, f32 = jnp.bfloat16, jnp.float32


def send(value, move, only=None):
    pairs = []
    for i in range(int(np.prod(SIZES))):
        at = dict(zip(AXES, (int(v) for v in np.unravel_index(i, SIZES))))
        if only is None or only(at):
            to = {**at, **move(at)}
            pairs.append((i, int(np.ravel_multi_index([to[a] for a in AXES], SIZES))))
    return lax.ppermute(value, AXES, pairs)


def along(axis, k):
    return lambda at: {axis: (at[axis] + k) % 4}


def gram_kernel(stride, rows, at_ref, a1_ref, a2_ref, b1_ref, b2_ref, *outs):
    z, x, base = at_ref[0], at_ref[1], at_ref[2]
    n = outs[0].shape[1]
    for half in range(2):
        for k in range(4):
            picks1, picks2 = [], []
            for j in range(4):
                dx, dz = (k, j) if half == 0 else (j, k)
                block = lax.rem(z + dz, 4) * 4 + lax.rem(x + dx, 4)
                start = pl.ds(pl.multiple_of(block * stride + base, rows), rows)
                picks1.append(a1_ref[start, :])
                picks2.append(a2_ref[start, :])
            left1, left2 = jnp.concatenate(picks1), jnp.concatenate(picks2)
            cols = pl.ds(half * n, n)
            nt = (((1,), (1,)), ((), ()))
            acc = lax.dot_general(left1, b1_ref[cols, :], nt, preferred_element_type=f32)
            acc += lax.dot_general(left2, b2_ref[cols, :], nt, preferred_element_type=f32)
            outs[4 * half + k][...] = acc.astype(bf16)


def gram(at, a1, a2, b1, b2, stride, rows):
    n = b1.shape[0] // 2
    vmem = pl.BlockSpec(memory_space=pltpu.VMEM)
    flops = 4 * 16 * rows * b1.shape[0] * b1.shape[1]
    return pl.pallas_call(
        functools.partial(gram_kernel, stride, rows),
        out_shape=[jax.ShapeDtypeStruct((4 * rows, n), bf16)] * 8,
        in_specs=[pl.BlockSpec(memory_space=pltpu.SMEM)] + [vmem] * 4,
        out_specs=[vmem] * 8,
        cost_estimate=pl.CostEstimate(flops=flops, bytes_accessed=10 << 20, transcendentals=0),
    )(at, a1, a2, b1, b2)


def scatter_sum(parts, rows):
    got = []
    for half, axis in ((0, "x"), (1, "z")):
        got.append([send(parts[4 * half + k], along(axis, k)) for k in (1, 2, 3)])
    mids = []
    for half in range(2):
        mids.append([])
        for j in range(4):
            cut = lambda v: lax.slice_in_dim(v, j * rows, (j + 1) * rows).astype(f32)
            total = cut(parts[4 * half])
            for r in got[half]:
                total = total + cut(r)
            mids[half].append(total)
    sums = []
    for half, axis in ((0, "z"), (1, "x")):
        total = mids[half][0]
        rs = [send(mids[half][k].astype(bf16), along(axis, k)) for k in (1, 2, 3)]
        for r in rs:
            total = total + r.astype(f32)
        sums.append(total)
    return jnp.concatenate(sums, axis=1)


def on_device(grads, covariance, test_grads, inverse_factor):
    tokens, feats = grads.shape
    z, x, c = lax.axis_index("z"), lax.axis_index("x"), lax.axis_index("c")
    yl, h = lax.axis_index("yl"), lax.axis_index("yh")
    rows = feats // 32
    gt = grads.T
    blocks = gt.reshape(16, 2, rows, tokens)
    pick = lambda v, i: lax.dynamic_index_in_dim(v, i, 1, keepdims=False).reshape(16 * rows, tokens)
    mine, other = pick(blocks, c), pick(blocks, 1 - c)
    b_same = send(mine, lambda at: {"yh": 1 - at["yh"]})
    b_flip = send(other, lambda at: {"yh": 1 - at["yh"], "c": 1 - at["c"]})
    sib = send(gt, lambda at: {"c": 1 - at["c"]})

    tt = test_grads.T
    slots = inverse_factor.reshape(rows, 32, 2 * rows).transpose(1, 0, 2)
    slots = jnp.concatenate([slots, jnp.broadcast_to(tt[None], (32,) + tt.shape)], axis=2)
    slots = lax.all_to_all(slots, ("yl", "z", "x"), split_axis=0, concat_axis=0, tiled=True)
    slots = slots.reshape(32 * rows, -1)
    pt = lax.dot_general(
        slots[:, : 2 * rows], slots[:, 2 * rows :], (((0,), (0,)), ((), ())), preferred_element_type=f32
    )
    pt_keep = lax.dynamic_slice_in_dim(pt, c * rows, rows, 0)
    pt_give = lax.dynamic_slice_in_dim(pt, (1 - c) * rows, rows, 0)
    pt = (pt_keep + send(pt_give, lambda at: {"c": 1 - at["c"]})).astype(bf16)
    pt = jnp.broadcast_to(pt[None], (32,) + pt.shape)
    pt = lax.all_to_all(pt, ("yl", "z", "x"), split_axis=0, concat_axis=0, tiled=True)
    pt = pt.reshape(2, 16 * rows, -1)
    pt_own = lax.dynamic_index_in_dim(pt, h, 0, keepdims=False)
    pt_cross = lax.dynamic_index_in_dim(pt, 1 - h, 0, keepdims=False)

    at_own = jnp.stack([z, x, c * rows]).astype(jnp.int32)
    at_cross = jnp.stack([z, x, 0 * c]).astype(jnp.int32)
    own = scatter_sum(gram(at_own, gt, sib, gt, sib, 2 * rows, rows), rows)
    flip_yl = lambda at: {"yl": 1 - at["yl"]}
    own_in = send(own.astype(bf16), flip_yl, lambda at: at["yl"] != at["yh"])
    own = own + own_in.astype(f32)
    cross = scatter_sum(gram(at_cross, b_same, b_flip, gt, sib, rows, rows), rows)
    cross_in = send(cross.astype(bf16), flip_yl, lambda at: at["yl"] == at["yh"])
    cross = cross + cross_in.astype(f32)
    examples = tokens * 64
    covariance_out = 0.9 * covariance + jnp.where(yl == h, own, cross) / examples

    tn = (((0,), (0,)), ((), ()))
    dot = lambda a, b: lax.dot_general(a, b, tn, preferred_element_type=f32)
    sib_mine = pick(sib.reshape(16, 2, rows, tokens), c)
    s_keep = dot(mine, pt_own) + dot(b_same, pt_cross)
    s_give = dot(sib_mine, pt_own) + dot(b_flip, pt_cross)
    scores = s_keep + send(s_give, lambda at: {"c": 1 - at["c"]})
    return scores, covariance_out


def solution(mesh):
    grid = Mesh(mesh.devices.reshape(SIZES), AXES)
    return jax.shard_map(
        on_device,
        mesh=grid,
        in_specs=(P(DP, "yh"), P(DP, "yh"), P("yh", DP), P(DP, None)),
        out_specs=(P(DP, "yh"), P(DP, "yh")),
        check_vma=False,
    )
```

```python
import functools

import jax
import jax.numpy as jnp
import numpy as np
from jax import lax
from jax.experimental import pallas as pl
from jax.experimental.pallas import tpu as pltpu
from jax.sharding import Mesh
from jax.sharding import PartitionSpec as P

AXES = ("yl", "z", "x", "c", "yh")
SIZES = (2, 4, 4, 2, 2)
DP = ("yl", "z", "x", "c")
CHUNKS = ((0, 32), (32, 64))
NT = (((1,), (1,)), ((), ()))
TN = (((0,), (0,)), ((), ()))
bf16, f32 = jnp.bfloat16, jnp.float32
VMEM = pl.BlockSpec(memory_space=pltpu.VMEM)
SMEM = pl.BlockSpec(memory_space=pltpu.SMEM)


def send(value, move, only=None):
    pairs = []
    for i in range(int(np.prod(SIZES))):
        at = dict(zip(AXES, (int(v) for v in np.unravel_index(i, SIZES))))
        if only is None or only(at):
            to = {**at, **move(at)}
            pairs.append((i, int(np.ravel_multi_index([to[a] for a in AXES], SIZES))))
    return lax.ppermute(value, AXES, pairs)


def along(axis, k):
    return lambda at: {axis: (at[axis] + k) % 4}


def flip(*axes):
    return lambda at: {a: 1 - at[a] for a in axes}


def cross_kernel(rows, at_ref, a1_ref, a2_ref, b1_ref, b2_ref, *outs):
    z, x = at_ref[0], at_ref[1]
    n = outs[0].shape[1]
    for half in range(2):
        for k in range(4):
            picks1, picks2 = [], []
            for j in range(4):
                dx, dz = (k, j) if half == 0 else (j, k)
                block = lax.rem(z + dz, 4) * 4 + lax.rem(x + dx, 4)
                start = pl.ds(pl.multiple_of(block * rows, rows), rows)
                picks1.append(a1_ref[start, :])
                picks2.append(a2_ref[start, :])
            left1, left2 = jnp.concatenate(picks1), jnp.concatenate(picks2)
            cols = pl.ds(half * n, n)
            acc = lax.dot_general(left1, b1_ref[cols, :], NT, preferred_element_type=f32)
            acc += lax.dot_general(left2, b2_ref[cols, :], NT, preferred_element_type=f32)
            outs[4 * half + k][...] = acc.astype(bf16)


def cross_gram(at, a1, a2, b1, b2, rows):
    n = b1.shape[0] // 2
    return pl.pallas_call(
        functools.partial(cross_kernel, rows),
        out_shape=[jax.ShapeDtypeStruct((4 * rows, n), bf16)] * 8,
        in_specs=[SMEM] + [VMEM] * 4,
        out_specs=[VMEM] * 8,
        cost_estimate=pl.CostEstimate(
            flops=4 * 16 * rows * b1.shape[0] * b1.shape[1], bytes_accessed=8 << 20, transcendentals=0
        ),
    )(at, a1, a2, b1, b2)


def own_kernel(at_ref, b1_ref, b2_ref, out_ref):
    base = at_ref[0]
    rows = out_ref.shape[1]
    wide = 2 * rows
    for g in range(4):
        starts = [pl.ds(pl.multiple_of((4 * g + i) * wide + base, rows), rows) for i in range(4)]
        left1 = jnp.concatenate([b1_ref[s, :] for s in starts])
        left2 = jnp.concatenate([b2_ref[s, :] for s in starts])
        for q in range(3):
            cols = pl.ds((g + q) % 4 * 4 * wide, 4 * wide)
            acc = lax.dot_general(left1, b1_ref[cols, :], NT, preferred_element_type=f32)
            acc += lax.dot_general(left2, b2_ref[cols, :], NT, preferred_element_type=f32)
            acc = acc.astype(bf16)
            for i in range(4):
                lo, hi = max(4 * q, i), min(4 * q + 4, i + 9)
                if lo < hi:
                    piece = acc[i * rows : (i + 1) * rows, (lo - 4 * q) * wide : (hi - 4 * q) * wide]
                    out_ref[4 * g + i, :, (lo - i) * wide : (hi - i) * wide] = piece


def own_gram(at, b1, b2, rows):
    return pl.pallas_call(
        own_kernel,
        out_shape=jax.ShapeDtypeStruct((16, rows, 18 * rows), bf16),
        in_specs=[SMEM, VMEM, VMEM],
        out_specs=VMEM,
        cost_estimate=pl.CostEstimate(
            flops=3 * 16 * rows * b1.shape[0] * b1.shape[1], bytes_accessed=6 << 20, transcendentals=0
        ),
    )(at, b1, b2)


def scatter_sum(parts, rows):
    got = []
    for half, axis in ((0, "x"), (1, "z")):
        got.append([send(parts[4 * half + k], along(axis, k)) for k in (1, 2, 3)])
    mids = []
    for half in range(2):
        mids.append([])
        for j in range(4):
            cut = lambda v: lax.slice_in_dim(v, j * rows, (j + 1) * rows).astype(f32)
            total = cut(parts[4 * half])
            for r in got[half]:
                total = total + cut(r)
            mids[half].append(total)
    sums = []
    for half, axis in ((0, "z"), (1, "x")):
        total = mids[half][0]
        rs = [send(mids[half][k].astype(bf16), along(axis, k)) for k in (1, 2, 3)]
        for r in rs:
            total = total + r.astype(f32)
        sums.append(total)
    return jnp.concatenate(sums, axis=1)


def gather_plane(block, z, x):
    zs = jnp.stack([block] + [send(block, along("z", -k)) for k in (1, 2, 3)])
    zs = jnp.roll(zs, z, axis=0)
    xs = jnp.stack([zs] + [send(zs, along("x", -k)) for k in (1, 2, 3)])
    xs = jnp.roll(xs, x, axis=0)
    return xs.transpose(1, 0, 2, 3).reshape((16,) + block.shape)


def on_device(grads, covariance, test_grads, inverse_factor):
    tokens, feats = grads.shape
    z, x, c = lax.axis_index("z"), lax.axis_index("x"), lax.axis_index("c")
    yl, h = lax.axis_index("yl"), lax.axis_index("yh")
    rows = feats // 32
    gt = grads.T
    pick = lambda v, i: lax.dynamic_index_in_dim(v.reshape(16, 2, rows, tokens), i, 1, keepdims=False)
    cut = lambda v, lo, hi: v[:, lo:hi].reshape(16 * (hi - lo), tokens)
    mine, other = pick(gt, c), pick(gt, 1 - c)
    sib = send(gt, flip("c"))
    arrived = []
    for lo, hi in CHUNKS:
        a, b = cut(mine, lo, hi), cut(other, lo, hi)
        if arrived:
            a, b, _ = lax.optimization_barrier((a, b, arrived[-1]))
        arrived.append((send(a, flip("yh")), send(b, flip("yh", "c"))))

    test_grads, inverse_factor, mine = lax.optimization_barrier((test_grads, inverse_factor, mine))
    tt = test_grads.T
    slots = inverse_factor.reshape(rows, 2, 16, 2 * rows).transpose(2, 0, 1, 3).reshape(16, rows, 4 * rows)
    slots = jnp.concatenate([slots, jnp.broadcast_to(tt[None], (16,) + tt.shape)], axis=2)
    slots = lax.all_to_all(slots, ("z", "x"), split_axis=0, concat_axis=0, tiled=True)
    slots = slots.reshape(16 * rows, -1)
    pt = lax.dot_general(slots[:, : 4 * rows], slots[:, 4 * rows :], TN, preferred_element_type=f32)
    pt = pt.reshape(4, rows, -1)
    at = lambda a, b: lax.dynamic_index_in_dim(pt, 2 * a + b, 0, keepdims=False)
    pt = (
        at(yl, c)
        + send(at(yl, 1 - c), flip("c"))
        + send(at(1 - yl, c), flip("yl"))
        + send(at(1 - yl, 1 - c), flip("yl", "c"))
    ).astype(bf16)
    far = send(pt, flip("yl"))
    pt = jnp.concatenate([jnp.where(yl == 0, pt, far), jnp.where(yl == 0, far, pt)], axis=0)
    pt = gather_plane(pt, z, x).reshape(16, 2, rows, -1)
    pt_own = lax.dynamic_index_in_dim(pt, h, 1, keepdims=False)
    pt_cross = lax.dynamic_index_in_dim(pt, 1 - h, 1, keepdims=False)

    own_parts = own_gram(jnp.stack([c * rows]).astype(jnp.int32), gt, sib, rows)
    token = own_parts[0, :8, :128]
    own = lax.all_to_all(own_parts, ("z", "x"), split_axis=0, concat_axis=0, tiled=True)
    own = own.astype(f32).sum(axis=0)
    own = own + send(own.astype(bf16), flip("yl"), lambda at: at["yl"] != at["yh"]).astype(f32)
    chip = z * 4 + x
    wide = jnp.concatenate([own, jnp.zeros((rows, 14 * rows), f32)], axis=1).reshape(rows, 16, 2 * rows)
    direct = jnp.roll(wide, chip, axis=1)
    mirror = direct.astype(bf16).transpose(1, 0, 2)
    mirror = lax.all_to_all(mirror, ("z", "x"), split_axis=0, concat_axis=0, tiled=True)
    mirror = mirror.reshape(16 * rows, 2 * rows).T
    keep = lax.dynamic_slice_in_dim(mirror, c * rows, rows, 0)
    give = lax.dynamic_slice_in_dim(mirror, (1 - c) * rows, rows, 0)
    far = send(give, flip("c"))
    both = [jnp.where(c == 0, keep, far), jnp.where(c == 0, far, keep)]
    both = jnp.stack([v.reshape(rows, 16, rows) for v in both], axis=2).reshape(rows, 16, 2 * rows)
    near = (lax.broadcasted_iota(jnp.int32, (rows, 16, 2 * rows), 1) - chip) % 16 <= 8
    own = jnp.where(near, direct, both.astype(f32)).reshape(rows, feats)

    at_zx = jnp.stack([z, x]).astype(jnp.int32)
    cross = []
    for (lo, hi), (a1, a2) in zip(CHUNKS, arrived):
        a1, a2, _ = lax.optimization_barrier((a1, a2, token))
        part = scatter_sum(cross_gram(at_zx, a1, a2, gt, sib, hi - lo), hi - lo)
        far = send(part.astype(bf16), flip("yl"), lambda at: at["yl"] == at["yh"])
        cross.append(part + far.astype(f32))
    cross = jnp.concatenate(cross, axis=0)
    examples = tokens * 64
    covariance_out = 0.9 * covariance + jnp.where(yl == h, own, cross) / examples

    dot = lambda a, b: lax.dot_general(a, b, TN, preferred_element_type=f32)
    flat = lambda v: v.reshape(-1, v.shape[-1])
    s_keep = dot(flat(mine), flat(pt_own))
    s_give = dot(flat(pick(sib, c)), flat(pt_own))
    for (lo, hi), (a1, a2) in zip(CHUNKS, arrived):
        s_keep += dot(a1, flat(pt_cross[:, lo:hi]))
        s_give += dot(a2, flat(pt_cross[:, lo:hi]))
    scores = s_keep + send(s_give, flip("c"))
    return scores, covariance_out


def solution(mesh):
    grid = Mesh(mesh.devices.reshape(SIZES), AXES)
    return jax.shard_map(
        on_device,
        mesh=grid,
        in_specs=(P(DP, "yh"), P(DP, "yh"), P("yh", DP), P(DP, None)),
        out_specs=(P(DP, "yh"), P(DP, "yh")),
        check_vma=False,
    )
```

```python
import functools

import jax
import jax.numpy as jnp
import numpy as np
from jax import lax
from jax.experimental import pallas as pl
from jax.experimental.pallas import tpu as pltpu
from jax.sharding import Mesh
from jax.sharding import PartitionSpec as P

AXES = ("yl", "z", "x", "c", "yh")
SIZES = (2, 4, 4, 2, 2)
DP = ("yl", "z", "x", "c")
CHUNKS = ((0, 32, "z", "x"), (32, 64, "x", "z"))
NT = (((1,), (1,)), ((), ()))
TN = (((0,), (0,)), ((), ()))
bf16, f32 = jnp.bfloat16, jnp.float32
VMEM = pl.BlockSpec(memory_space=pltpu.VMEM)
ANY = pl.BlockSpec(memory_space=pl.ANY)
SMEM = pl.BlockSpec(memory_space=pltpu.SMEM)


def send(value, move, only=None):
    pairs = []
    for i in range(int(np.prod(SIZES))):
        at = dict(zip(AXES, (int(v) for v in np.unravel_index(i, SIZES))))
        if only is None or only(at):
            to = {**at, **move(at)}
            pairs.append((i, int(np.ravel_multi_index([to[a] for a in AXES], SIZES))))
    return lax.ppermute(value, AXES, pairs)


def along(axis, k):
    return lambda at: {axis: (at[axis] + k) % 4}


def flip(*axes):
    return lambda at: {a: 1 - at[a] for a in axes}


def kernel_call(body, outs, specs, *args, flops=0):
    nbytes = sum(a.size * a.dtype.itemsize for a in args) + sum(o.size * o.dtype.itemsize for o in outs)
    return pl.pallas_call(
        body,
        out_shape=outs,
        in_specs=specs,
        out_specs=[VMEM] * len(outs),
        cost_estimate=pl.CostEstimate(flops=flops, bytes_accessed=nbytes, transcendentals=0),
    )(*args)


def slots_kernel(f_ref, t_ref, out_ref):
    wide = f_ref.shape[1] // 32
    for s in range(16):
        out_ref[s, :, :wide] = f_ref[:, s * wide : (s + 1) * wide]
        out_ref[s, :, wide : 2 * wide] = f_ref[:, (16 + s) * wide : (17 + s) * wide]
        out_ref[s, :, 2 * wide :] = t_ref[...]


def factor_kernel(wide, slots_ref, after_ref, also_ref, out_ref):
    out_ref[...] = lax.dot_general(
        slots_ref[:, :wide], slots_ref[:, wide:], TN, preferred_element_type=f32
    )


def pick_kernel(at_ref, gt_ref, sib_ref, *outs):
    for (lo, hi, _, _), out_ref in zip(CHUNKS, outs):
        n = hi - lo
        for b in range(16):
            start = pl.ds(pl.multiple_of(b * 128 + at_ref[2] + lo, 16), n)
            out_ref[b * n : (b + 1) * n, :] = gt_ref[start, :]
            out_ref[(16 + b) * n : (17 + b) * n, :] = sib_ref[start, :]


def gram_kernel(rows, stride, z_first, at_ref, a1_ref, a2_ref, b1_ref, b2_ref, after_ref, *outs):
    z, x, base = at_ref[0], at_ref[1], at_ref[2]
    starts = []
    for k in range(4):
        for j in range(4):
            dz, dx = (k, j) if z_first else (j, k)
            block = lax.rem(z + dz, 4) * 4 + lax.rem(x + dx, 4)
            starts.append(pl.ds(pl.multiple_of(block * stride + base, rows), rows))
    left1 = jnp.concatenate([a1_ref[s, :] for s in starts])
    left2 = jnp.concatenate([a2_ref[s, :] for s in starts])
    tile = 256
    for n in range(b1_ref.shape[0] // tile):
        cols = pl.ds(n * tile, tile)
        acc = lax.dot_general(left1, b1_ref[cols, :], NT, preferred_element_type=f32)
        acc += lax.dot_general(left2, b2_ref[cols, :], NT, preferred_element_type=f32)
        for k in range(4):
            outs[k][:, cols] = acc[4 * k * rows : 4 * (k + 1) * rows].astype(bf16)


def gram(at, a1, a2, b1, b2, after, rows, stride, first):
    n = b1.shape[0]
    return kernel_call(
        functools.partial(gram_kernel, rows, stride, first == "z"),
        [jax.ShapeDtypeStruct((4 * rows, n), bf16)] * 4,
        [SMEM] + [VMEM] * 4 + [ANY],
        at, a1, a2, b1, b2, after,
        flops=4 * 16 * rows * n * b1.shape[1],
    )


def scores_kernel(at_ref, pt_ref, *refs):
    h = at_ref[3]
    n = len(CHUNKS)
    own, cross, (keep_ref, give_ref) = refs[:n], refs[n : 2 * n], refs[2 * n :]
    for side, out_ref in enumerate((keep_ref, give_ref)):
        acc = None
        for which, group in ((h, own), (1 - h, cross)):
            for (lo, hi, _, _), ref in zip(CHUNKS, group):
                m = 16 * (hi - lo)
                p = pt_ref[:, pl.ds(which, 1), lo:hi, :].reshape(m, pt_ref.shape[-1])
                d = lax.dot_general(ref[side * m : (side + 1) * m, :], p, TN, preferred_element_type=f32)
                acc = d if acc is None else acc + d
        out_ref[...] = acc


def first_stage(parts, rows, axis):
    got = [send(parts[k], along(axis, k)) for k in (1, 2, 3)]
    mids = []
    for j in range(4):
        cut = lambda v: lax.slice_in_dim(v, j * rows, (j + 1) * rows).astype(f32)
        mids.append(cut(parts[0]) + cut(got[0]) + cut(got[1]) + cut(got[2]))
    return mids


def second_stage(mids, axis):
    got = [send(mids[k].astype(bf16), along(axis, k)) for k in (1, 2, 3)]
    return mids[0] + got[0].astype(f32) + got[1].astype(f32) + got[2].astype(f32)


def on_device(grads, covariance, test_grads, inverse_factor):
    tokens, feats = grads.shape
    z, x, c = lax.axis_index("z"), lax.axis_index("x"), lax.axis_index("c")
    yl, h = lax.axis_index("yl"), lax.axis_index("yh")
    rows = feats // 32
    tests = test_grads.shape[0]
    at = jnp.stack([z, x, c * rows, h]).astype(jnp.int32)
    at_cross = jnp.stack([z, x, 0 * c, h]).astype(jnp.int32)
    shape = jax.ShapeDtypeStruct
    gt = grads.T
    sib = send(gt, flip("c"))

    picked = kernel_call(
        pick_kernel,
        [shape((32 * (hi - lo), tokens), bf16) for lo, hi, _, _ in CHUNKS],
        [SMEM, VMEM, VMEM],
        at, gt, sib,
    )
    arrived = [send(a, flip("yh")) for a in picked]
    own = gram(at, gt, sib, gt, sib, picked[0], rows, 2 * rows, "x")

    (slots,) = kernel_call(
        slots_kernel,
        [shape((16, rows, 4 * rows + tests), bf16)],
        [VMEM, VMEM],
        inverse_factor, test_grads.T,
    )
    slots = lax.all_to_all(slots, ("z", "x"), split_axis=0, concat_axis=0, tiled=True)
    (pt,) = kernel_call(
        functools.partial(factor_kernel, 4 * rows),
        [shape((4 * rows, tests), f32)],
        [VMEM, ANY, ANY],
        slots.reshape(16 * rows, -1), own[0], arrived[0],
        flops=2 * 16 * rows * 4 * rows * tests,
    )
    pt = pt.reshape(2, 2, rows, tests)
    half = lambda i: lax.dynamic_index_in_dim(pt, i, 1, keepdims=False)
    pt = half(c) + send(half(1 - c), flip("c"))
    pt = (pt + send(pt, flip("yl"))).astype(bf16)
    pt = jnp.broadcast_to(pt[None], (16,) + pt.shape)
    pt = lax.all_to_all(pt, ("z", "x"), split_axis=0, concat_axis=0, tiled=True)

    after = own[0]
    own = second_stage(first_stage(own, rows, "x"), "z")
    own = own + send(own.astype(bf16), flip("yl"), lambda at: at["yl"] != at["yh"]).astype(f32)

    cross = []
    for (lo, hi, first, second), a in zip(CHUNKS, arrived):
        n, m = hi - lo, a.shape[0] // 2
        parts = gram(at_cross, a[:m], a[m:], gt, sib, after, n, n, first)
        after = parts[0]
        part = second_stage(first_stage(parts, n, first), second)
        far = send(part.astype(bf16), flip("yl"), lambda at: at["yl"] == at["yh"])
        cross.append(part + far.astype(f32))
    cross = jnp.concatenate(cross, axis=0)
    examples = tokens * 64
    covariance_out = 0.9 * covariance + jnp.where(yl == h, own, cross) / examples

    keep, give = kernel_call(
        scores_kernel,
        [shape((tokens, tests), f32)] * 2,
        [SMEM] + [VMEM] * (1 + 2 * len(CHUNKS)),
        at, pt, *picked, *arrived,
        flops=8 * 16 * rows * tokens * tests,
    )
    return keep + send(give, flip("c")), covariance_out


def solution(mesh):
    grid = Mesh(mesh.devices.reshape(SIZES), AXES)
    return jax.shard_map(
        on_device,
        mesh=grid,
        in_specs=(P(DP, "yh"), P(DP, "yh"), P("yh", DP), P(DP, None)),
        out_specs=(P(DP, "yh"), P(DP, "yh")),
        check_vma=False,
    )
```

```python
import functools

import jax
import jax.numpy as jnp
import numpy as np
from jax import lax
from jax.experimental import pallas as pl
from jax.experimental.pallas import tpu as pltpu
from jax.sharding import Mesh
from jax.sharding import PartitionSpec as P

AXES = ("yl", "z", "x", "c", "yh")
SIZES = (2, 4, 4, 2, 2)
DP = ("yl", "z", "x", "c")
CHUNKS = ((0, 32), (32, 64))
OWN_AXES = (("x", "z"), ("z", "x"))
CROSS_AXES = (("z", "x"), ("x", "z"))
NT = (((1,), (1,)), ((), ()))
TN = (((0,), (0,)), ((), ()))
bf16, f32 = jnp.bfloat16, jnp.float32
VMEM = pl.BlockSpec(memory_space=pltpu.VMEM)
ANY = pl.BlockSpec(memory_space=pl.ANY)
SMEM = pl.BlockSpec(memory_space=pltpu.SMEM)


def send(value, move, only=None):
    pairs = []
    for i in range(int(np.prod(SIZES))):
        at = dict(zip(AXES, (int(v) for v in np.unravel_index(i, SIZES))))
        if only is None or only(at):
            to = {**at, **move(at)}
            pairs.append((i, int(np.ravel_multi_index([to[a] for a in AXES], SIZES))))
    return lax.ppermute(value, AXES, pairs)


def along(axis, k):
    return lambda at: {axis: (at[axis] + k) % 4}


def flip(*axes):
    return lambda at: {a: 1 - at[a] for a in axes}


def kernel_call(body, outs, specs, *args, flops=0):
    nbytes = sum(a.size * a.dtype.itemsize for a in args) + sum(o.size * o.dtype.itemsize for o in outs)
    return pl.pallas_call(
        body,
        out_shape=outs,
        in_specs=specs,
        out_specs=[VMEM] * len(outs),
        cost_estimate=pl.CostEstimate(flops=flops, bytes_accessed=nbytes, transcendentals=0),
    )(*args)


def slots_kernel(f_ref, t_ref, out_ref):
    wide = f_ref.shape[1] // 32
    for s in range(16):
        out_ref[s, :, :wide] = f_ref[:, s * wide : (s + 1) * wide]
        out_ref[s, :, wide : 2 * wide] = f_ref[:, (16 + s) * wide : (17 + s) * wide]
        out_ref[s, :, 2 * wide :] = t_ref[...]


def factor_kernel(wide, slots_ref, after_ref, also_ref, out_ref):
    out_ref[...] = lax.dot_general(
        slots_ref[:, :wide], slots_ref[:, wide:], TN, preferred_element_type=f32
    )


def copy_rows(src_ref, base, lo, hi, out_ref, first):
    n = hi - lo
    for b in range(16):
        start = pl.ds(pl.multiple_of(b * 128 + base + lo, 16), n)
        out_ref[first + b * n : first + (b + 1) * n, :] = src_ref[start, :]


def pick_mine_kernel(at_ref, gt_ref, one_ref, two_ref):
    for chunk, out_ref in zip(CHUNKS, (one_ref, two_ref)):
        copy_rows(gt_ref, at_ref[2], *chunk, out_ref, 0)


def pick_both_kernel(at_ref, two_ref, sib_ref, one_out, two_out):
    copy_rows(sib_ref, at_ref[2], *CHUNKS[0], one_out, 0)
    m = two_ref.shape[0]
    two_out[:m, :] = two_ref[...]
    copy_rows(sib_ref, at_ref[2], *CHUNKS[1], two_out, m)


def gram_kernel(rows, stride, lo, z_first, at_ref, a1_ref, a2_ref, b1_ref, b2_ref, after_ref, *outs):
    z, x, base1, base2 = at_ref[0], at_ref[1], at_ref[2], at_ref[3]
    left1, left2 = [], []
    for k in range(4):
        for j in range(4):
            dz, dx = (k, j) if z_first else (j, k)
            block = (lax.rem(z + dz, 4) * 4 + lax.rem(x + dx, 4)) * stride + lo
            left1.append(a1_ref[pl.ds(pl.multiple_of(block + base1, rows), rows), :])
            left2.append(a2_ref[pl.ds(pl.multiple_of(block + base2, rows), rows), :])
    left1, left2 = jnp.concatenate(left1), jnp.concatenate(left2)
    tile = 256
    for n in range(b1_ref.shape[0] // tile):
        cols = pl.ds(n * tile, tile)
        acc = lax.dot_general(left1, b1_ref[cols, :], NT, preferred_element_type=f32)
        acc += lax.dot_general(left2, b2_ref[cols, :], NT, preferred_element_type=f32)
        for k in range(4):
            outs[k][:, cols] = acc[4 * k * rows : 4 * (k + 1) * rows].astype(bf16)


def gram(at, a1, a2, b1, b2, after, rows, stride, lo, first):
    n = b1.shape[0]
    return kernel_call(
        functools.partial(gram_kernel, rows, stride, lo, first == "z"),
        [jax.ShapeDtypeStruct((4 * rows, n), bf16)] * 4,
        [SMEM] + [VMEM] * 4 + [ANY],
        at, a1, a2, b1, b2, after,
        flops=4 * 16 * rows * n * b1.shape[1],
    )


def scores_kernel(at_ref, pt_ref, *refs):
    h = at_ref[4]
    keep_ref, give_ref = refs[6:]
    for side, out_ref in enumerate((keep_ref, give_ref)):
        acc = None
        for which, group in ((h, refs[:3]), (1 - h, refs[3:6])):
            m = group[0].shape[0]
            lefts = (group[side][...], group[2][side * m : (side + 1) * m, :])
            for (lo, hi), left in zip(CHUNKS, lefts):
                p = pt_ref[:, pl.ds(which, 1), lo:hi, :].reshape(m, pt_ref.shape[-1])
                d = lax.dot_general(left, p, TN, preferred_element_type=f32)
                acc = d if acc is None else acc + d
        out_ref[...] = acc


def sum_kernel(mine_ref, g1_ref, g2_ref, g3_ref, after_ref, out_ref):
    out_ref[...] = mine_ref[...] + g1_ref[...].astype(f32) + g2_ref[...].astype(f32) + g3_ref[...].astype(f32)


def first_stage(parts, rows, axis):
    got = [send(parts[k], along(axis, k)) for k in (1, 2, 3)]
    mids = []
    for j in range(4):
        cut = lambda v: lax.slice_in_dim(v, j * rows, (j + 1) * rows).astype(f32)
        mids.append(cut(parts[0]) + cut(got[0]) + cut(got[1]) + cut(got[2]))
    return mids


def second_stage(mids, axis, after=None):
    got = [send(mids[k].astype(bf16), along(axis, k)) for k in (1, 2, 3)]
    if after is not None:
        out = jax.ShapeDtypeStruct(mids[0].shape, f32)
        return kernel_call(sum_kernel, [out], [VMEM] * 4 + [ANY], mids[0], *got, after)[0]
    return mids[0] + got[0].astype(f32) + got[1].astype(f32) + got[2].astype(f32)


def on_device(grads, covariance, test_grads, inverse_factor):
    tokens, feats = grads.shape
    z, x, c = lax.axis_index("z"), lax.axis_index("x"), lax.axis_index("c")
    yl, h = lax.axis_index("yl"), lax.axis_index("yh")
    rows = feats // 32
    tests = test_grads.shape[0]
    zero = 0 * c
    at = jnp.stack([z, x, c * rows, c * rows, h]).astype(jnp.int32)
    at_cross = jnp.stack([z, x, zero, zero, h]).astype(jnp.int32)
    at_cross2 = jnp.stack([z, x, zero, zero + feats // 4, h]).astype(jnp.int32)
    shape = jax.ShapeDtypeStruct
    gt = grads.T
    sib = send(gt, flip("c"))

    part = shape((feats // 4, tokens), bf16)
    picked1, picked2 = kernel_call(pick_mine_kernel, [part] * 2, [SMEM, VMEM], at, gt)
    arrived1 = send(picked1, flip("yh"))
    picked3, picked4 = kernel_call(
        pick_both_kernel, [part, shape((feats // 2, tokens), bf16)], [SMEM, VMEM, VMEM], at, picked2, sib
    )
    arrived3, arrived4 = send(picked3, flip("yh")), send(picked4, flip("yh"))

    own, after = [], picked3
    for (lo, hi), (first, _) in zip(CHUNKS, OWN_AXES):
        own.append(gram(at, gt, sib, gt, sib, after, hi - lo, 2 * rows, lo, first))
        after = own[-1][0]
    n = rows // 2
    cross = [gram(at_cross, arrived1, arrived3, gt, sib, after, n, n, 0, CROSS_AXES[0][0])]
    cross.append(gram(at_cross2, arrived4, arrived4, gt, sib, cross[0][0], n, n, 0, CROSS_AXES[1][0]))

    (slots,) = kernel_call(
        slots_kernel,
        [shape((16, rows, 4 * rows + tests), bf16)],
        [VMEM, VMEM],
        inverse_factor, test_grads.T,
    )
    slots = lax.all_to_all(slots, ("z", "x"), split_axis=0, concat_axis=0, tiled=True)
    (pt,) = kernel_call(
        functools.partial(factor_kernel, 4 * rows),
        [shape((4 * rows, tests), f32)],
        [VMEM, ANY, ANY],
        slots.reshape(16 * rows, -1), own[1][0], arrived3,
        flops=2 * 16 * rows * 4 * rows * tests,
    )
    pt = pt.reshape(2, 2, rows, tests)
    half = lambda i: lax.dynamic_index_in_dim(pt, i, 1, keepdims=False)
    pt = half(c) + send(half(1 - c), flip("c"))
    pt = (pt + send(pt, flip("yl"))).astype(bf16)
    pt = jnp.broadcast_to(pt[None], (16,) + pt.shape)
    pt = lax.all_to_all(pt, ("z", "x"), split_axis=0, concat_axis=0, tiled=True)

    keep, give = kernel_call(
        scores_kernel,
        [shape((tokens, tests), f32)] * 2,
        [SMEM] + [VMEM] * 7,
        at, pt, picked1, picked3, picked4, arrived1, arrived3, arrived4,
        flops=8 * 16 * rows * tokens * tests,
    )
    scores = keep + send(give, flip("c"))

    sums = []
    for parts, axes, owner in ((own, OWN_AXES, True), (cross, CROSS_AXES, False)):
        done = []
        for i, (first, second) in enumerate(axes):
            last = not owner and i == 1
            total = second_stage(first_stage(parts[i], n, first), second, keep if last else None)
            far = send(total.astype(bf16), flip("yl"), lambda at: (at["yl"] != at["yh"]) == owner)
            done.append(total + far.astype(f32))
        sums.append(jnp.concatenate(done, axis=0))
    examples = tokens * 64
    covariance_out = 0.9 * covariance + jnp.where(yl == h, *sums) / examples
    return scores, covariance_out


def solution(mesh):
    grid = Mesh(mesh.devices.reshape(SIZES), AXES)
    return jax.shard_map(
        on_device,
        mesh=grid,
        in_specs=(P(DP, "yh"), P(DP, "yh"), P("yh", DP), P(DP, None)),
        out_specs=(P(DP, "yh"), P(DP, "yh")),
        check_vma=False,
    )
```

```python
import functools

import jax
import jax.numpy as jnp
import numpy as np
from jax import lax
from jax.experimental import pallas as pl
from jax.experimental.pallas import tpu as pltpu
from jax.sharding import Mesh
from jax.sharding import PartitionSpec as P

AXES = ("yl", "z", "x", "c", "yh")
SIZES = (2, 4, 4, 2, 2)
DP = ("yl", "z", "x", "c")
NT = (((1,), (1,)), ((), ()))
TN = (((0,), (0,)), ((), ()))
bf16, f32 = jnp.bfloat16, jnp.float32
VMEM = pl.BlockSpec(memory_space=pltpu.VMEM)
ANY = pl.BlockSpec(memory_space=pl.ANY)
SMEM = pl.BlockSpec(memory_space=pltpu.SMEM)


def send(value, move, only=None):
    pairs = []
    for i in range(int(np.prod(SIZES))):
        at = dict(zip(AXES, (int(v) for v in np.unravel_index(i, SIZES))))
        if only is None or only(at):
            to = {**at, **move(at)}
            pairs.append((i, int(np.ravel_multi_index([to[a] for a in AXES], SIZES))))
    return lax.ppermute(value, AXES, pairs)


def along(axis, k):
    return lambda at: {axis: (at[axis] + k) % 4}


def flip(*axes):
    return lambda at: {a: 1 - at[a] for a in axes}


def kernel_call(body, outs, specs, *args, flops=0):
    nbytes = sum(a.size * a.dtype.itemsize for a in args) + sum(o.size * o.dtype.itemsize for o in outs)
    return pl.pallas_call(
        body,
        out_shape=outs,
        in_specs=specs,
        out_specs=[VMEM] * len(outs),
        cost_estimate=pl.CostEstimate(flops=flops, bytes_accessed=nbytes, transcendentals=0),
    )(*args)


def slots_kernel(f_ref, t_ref, out_ref):
    wide = f_ref.shape[1] // 32
    for s in range(16):
        out_ref[s, :, :wide] = f_ref[:, s * wide : (s + 1) * wide]
        out_ref[s, :, wide : 2 * wide] = f_ref[:, (16 + s) * wide : (17 + s) * wide]
        out_ref[s, :, 2 * wide :] = t_ref[...]


def factor_kernel(wide, slots_ref, after_ref, also_ref, out_ref):
    out_ref[...] = lax.dot_general(
        slots_ref[:, :wide], slots_ref[:, wide:], TN, preferred_element_type=f32
    )


def pick_kernel(at_ref, gt_ref, sib_ref, out_ref):
    for i, ref in enumerate((gt_ref, sib_ref)):
        for b in range(16):
            start = pl.ds(pl.multiple_of(b * 128 + at_ref[2], 64), 64)
            out_ref[(16 * i + b) * 64 : (16 * i + b + 1) * 64, :] = ref[start, :]


def gram_kernel(at_ref, a_ref, b1_ref, b2_ref, after_ref, *outs):
    z, x = at_ref[0], at_ref[1]
    rows, m, n, tile = 64, a_ref.shape[0] // 2, b1_ref.shape[0] // 2, 256
    for half in range(2):
        left1, left2 = [], []
        for k in range(4):
            for j in range(4):
                dx, dz = (k, j) if half == 0 else (j, k)
                block = (lax.rem(z + dz, 4) * 4 + lax.rem(x + dx, 4)) * rows
                left1.append(a_ref[pl.ds(pl.multiple_of(block, rows), rows), :])
                left2.append(a_ref[pl.ds(pl.multiple_of(block + m, rows), rows), :])
        left1, left2 = jnp.concatenate(left1), jnp.concatenate(left2)
        for t in range(n // tile):
            cols = pl.ds(half * n + t * tile, tile)
            acc = lax.dot_general(left1, b1_ref[cols, :], NT, preferred_element_type=f32)
            acc += lax.dot_general(left2, b2_ref[cols, :], NT, preferred_element_type=f32)
            for k in range(4):
                part = acc[4 * k * rows : 4 * (k + 1) * rows].astype(bf16)
                outs[4 * half + k][:, t * tile : (t + 1) * tile] = part


def gram(at, a, b1, b2, after):
    n = b1.shape[0]
    return kernel_call(
        gram_kernel,
        [jax.ShapeDtypeStruct((256, n // 2), bf16)] * 8,
        [SMEM] + [VMEM] * 3 + [ANY],
        at, a, b1, b2, after,
        flops=2 * a.shape[0] * n * b1.shape[1],
    )


def scores_kernel(at_ref, pt_ref, own_ref, cross_ref, keep_ref, give_ref):
    h = at_ref[3]
    m = own_ref.shape[0] // 2
    p_own = pt_ref[:, pl.ds(h, 1), :, :].reshape(m, pt_ref.shape[-1])
    p_cross = pt_ref[:, pl.ds(1 - h, 1), :, :].reshape(m, pt_ref.shape[-1])
    for side, out_ref in enumerate((keep_ref, give_ref)):
        s = slice(side * m, (side + 1) * m)
        acc = lax.dot_general(own_ref[s, :], p_own, TN, preferred_element_type=f32)
        out_ref[...] = acc + lax.dot_general(cross_ref[s, :], p_cross, TN, preferred_element_type=f32)


def sum_kernel(mine_ref, g1_ref, g2_ref, g3_ref, after_ref, out_ref):
    out_ref[...] = mine_ref[...] + g1_ref[...].astype(f32) + g2_ref[...].astype(f32) + g3_ref[...].astype(f32)


def scatter_sum(parts, rows, after=None):
    got, mids, sums = [], [], []
    for half, axis in ((0, "x"), (1, "z")):
        got.append([send(parts[4 * half + k], along(axis, k)) for k in (1, 2, 3)])
    for half in range(2):
        mids.append([])
        for j in range(4):
            cut = lambda v: lax.slice_in_dim(v, j * rows, (j + 1) * rows).astype(f32)
            total = cut(parts[4 * half])
            for r in got[half]:
                total = total + cut(r)
            mids[half].append(total)
    for half, axis in ((0, "z"), (1, "x")):
        rs = [send(mids[half][k].astype(bf16), along(axis, k)) for k in (1, 2, 3)]
        if after is not None:
            out = jax.ShapeDtypeStruct(mids[half][0].shape, f32)
            sums.append(kernel_call(sum_kernel, [out], [VMEM] * 4 + [ANY], mids[half][0], *rs, after)[0])
        else:
            sums.append(mids[half][0] + rs[0].astype(f32) + rs[1].astype(f32) + rs[2].astype(f32))
    return jnp.concatenate(sums, axis=1)


def on_device(grads, covariance, test_grads, inverse_factor):
    tokens, feats = grads.shape
    z, x, c = lax.axis_index("z"), lax.axis_index("x"), lax.axis_index("c")
    yl, h = lax.axis_index("yl"), lax.axis_index("yh")
    rows = feats // 32
    tests = test_grads.shape[0]
    at = jnp.stack([z, x, c * rows, h]).astype(jnp.int32)
    shape = jax.ShapeDtypeStruct
    gt = grads.T
    sib = send(gt, flip("c"))

    (picked,) = kernel_call(pick_kernel, [shape((feats, tokens), bf16)], [SMEM, VMEM, VMEM], at, gt, sib)
    arrived = send(picked, flip("yh"))
    own = gram(at, picked, gt, sib, picked)
    cross = gram(at, arrived, gt, sib, own[0])

    (slots,) = kernel_call(
        slots_kernel,
        [shape((16, rows, 4 * rows + tests), bf16)],
        [VMEM, VMEM],
        inverse_factor, test_grads.T,
    )
    slots = lax.all_to_all(slots, ("z", "x"), split_axis=0, concat_axis=0, tiled=True)
    (pt,) = kernel_call(
        functools.partial(factor_kernel, 4 * rows),
        [shape((4 * rows, tests), f32)],
        [VMEM, ANY, ANY],
        slots.reshape(16 * rows, -1), own[0], arrived,
        flops=2 * 16 * rows * 4 * rows * tests,
    )
    pt = pt.reshape(2, 2, rows, tests)
    half = lambda i: lax.dynamic_index_in_dim(pt, i, 1, keepdims=False)
    pt = half(c) + send(half(1 - c), flip("c"))
    pt = (pt + send(pt, flip("yl"))).astype(bf16)
    pt = jnp.broadcast_to(pt[None], (16,) + pt.shape)
    pt = lax.all_to_all(pt, ("z", "x"), split_axis=0, concat_axis=0, tiled=True)

    keep, give = kernel_call(
        scores_kernel,
        [shape((tokens, tests), f32)] * 2,
        [SMEM] + [VMEM] * 3,
        at, pt, picked, arrived,
        flops=8 * 16 * rows * tokens * tests,
    )
    scores = keep + send(give, flip("c"))

    own = scatter_sum(own, rows)
    own = own + send(own.astype(bf16), flip("yl"), lambda at: at["yl"] != at["yh"]).astype(f32)
    cross = scatter_sum(cross, rows, keep)
    cross = cross + send(cross.astype(bf16), flip("yl"), lambda at: at["yl"] == at["yh"]).astype(f32)
    examples = tokens * 64
    covariance_out = 0.9 * covariance + jnp.where(yl == h, own, cross) / examples
    return scores, covariance_out


def solution(mesh):
    grid = Mesh(mesh.devices.reshape(SIZES), AXES)
    return jax.shard_map(
        on_device,
        mesh=grid,
        in_specs=(P(DP, "yh"), P(DP, "yh"), P("yh", DP), P(DP, None)),
        out_specs=(P(DP, "yh"), P(DP, "yh")),
        check_vma=False,
    )
```

```python
import functools

import jax
import jax.numpy as jnp
import numpy as np
from jax import lax
from jax.experimental import pallas as pl
from jax.experimental.pallas import tpu as pltpu
from jax.sharding import Mesh
from jax.sharding import PartitionSpec as P

AXES = ("yl", "z", "x", "c", "yh")
SIZES = (2, 4, 4, 2, 2)
DP = ("yl", "z", "x", "c")
NT = (((1,), (1,)), ((), ()))
TN = (((0,), (0,)), ((), ()))
bf16, f32 = jnp.bfloat16, jnp.float32
VMEM = pl.BlockSpec(memory_space=pltpu.VMEM)
ANY = pl.BlockSpec(memory_space=pl.ANY)
SMEM = pl.BlockSpec(memory_space=pltpu.SMEM)


def send(value, move, only=None):
    pairs = []
    for i in range(int(np.prod(SIZES))):
        at = dict(zip(AXES, (int(v) for v in np.unravel_index(i, SIZES))))
        if only is None or only(at):
            to = {**at, **move(at)}
            pairs.append((i, int(np.ravel_multi_index([to[a] for a in AXES], SIZES))))
    return lax.ppermute(value, AXES, pairs)


def along(axis, k):
    return lambda at: {axis: (at[axis] + k) % 4}


def flip(*axes):
    return lambda at: {a: 1 - at[a] for a in axes}


def kernel_call(body, outs, specs, *args, flops=0):
    nbytes = sum(a.size * a.dtype.itemsize for a in args) + sum(o.size * o.dtype.itemsize for o in outs)
    return pl.pallas_call(
        body,
        out_shape=outs,
        in_specs=specs,
        out_specs=[VMEM] * len(outs),
        cost_estimate=pl.CostEstimate(flops=flops, bytes_accessed=nbytes, transcendentals=0),
    )(*args)


def slots_kernel(f_ref, t_ref, out_ref):
    wide = f_ref.shape[1] // 32
    for s in range(16):
        out_ref[s, :, :wide] = f_ref[:, s * wide : (s + 1) * wide]
        out_ref[s, :, wide : 2 * wide] = f_ref[:, (16 + s) * wide : (17 + s) * wide]
        out_ref[s, :, 2 * wide :] = t_ref[...]


def factor_kernel(wide, slots_ref, after_ref, also_ref, out_ref):
    out_ref[...] = lax.dot_general(
        slots_ref[:, :wide], slots_ref[:, wide:], TN, preferred_element_type=f32
    )


def own_kernel(a1_ref, a2_ref, b1_ref, b2_ref, after_ref, out_ref):
    rows = out_ref.shape[1]
    wide = 2 * rows
    for g in range(4):
        left1 = a1_ref[4 * g * rows : 4 * (g + 1) * rows, :]
        left2 = a2_ref[4 * g * rows : 4 * (g + 1) * rows, :]
        for q in range(3):
            cols = pl.ds((g + q) % 4 * 4 * wide, 4 * wide)
            acc = lax.dot_general(left1, b1_ref[cols, :], NT, preferred_element_type=f32)
            acc += lax.dot_general(left2, b2_ref[cols, :], NT, preferred_element_type=f32)
            acc = acc.astype(bf16)
            for i in range(4):
                lo, hi = max(4 * q, i), min(4 * q + 4, i + 9)
                if lo < hi:
                    piece = acc[i * rows : (i + 1) * rows, (lo - 4 * q) * wide : (hi - 4 * q) * wide]
                    out_ref[4 * g + i, :, (lo - i) * wide : (hi - i) * wide] = piece


def gram_kernel(at_ref, a1_ref, a2_ref, b1_ref, b2_ref, after_ref, also_ref, *outs):
    z, x = at_ref[0], at_ref[1]
    rows, n, tile = 64, b1_ref.shape[0] // 2, 256
    for half in range(2):
        left1, left2 = [], []
        for k in range(4):
            for j in range(4):
                dx, dz = (k, j) if half == 0 else (j, k)
                block = (lax.rem(z + dz, 4) * 4 + lax.rem(x + dx, 4)) * rows
                start = pl.ds(pl.multiple_of(block, rows), rows)
                left1.append(a1_ref[start, :])
                left2.append(a2_ref[start, :])
        left1, left2 = jnp.concatenate(left1), jnp.concatenate(left2)
        for t in range(n // tile):
            cols = pl.ds(half * n + t * tile, tile)
            acc = lax.dot_general(left1, b1_ref[cols, :], NT, preferred_element_type=f32)
            acc += lax.dot_general(left2, b2_ref[cols, :], NT, preferred_element_type=f32)
            for k in range(4):
                part = acc[4 * k * rows : 4 * (k + 1) * rows].astype(bf16)
                outs[4 * half + k][:, t * tile : (t + 1) * tile] = part


def gram(at, a1, a2, b1, b2, after, also):
    n = b1.shape[0]
    return kernel_call(
        gram_kernel,
        [jax.ShapeDtypeStruct((256, n // 2), bf16)] * 8,
        [SMEM] + [VMEM] * 4 + [ANY] * 2,
        at, a1, a2, b1, b2, after, also,
        flops=4 * a1.shape[0] * n * b1.shape[1],
    )


def scores_kernel(at_ref, pt_ref, own1_ref, own2_ref, cross1_ref, cross2_ref, keep_ref, give_ref):
    h = at_ref[3]
    m = own1_ref.shape[0]
    p_own = pt_ref[:, pl.ds(h, 1), :, :].reshape(m, pt_ref.shape[-1])
    p_cross = pt_ref[:, pl.ds(1 - h, 1), :, :].reshape(m, pt_ref.shape[-1])
    for own, cross, out_ref in ((own1_ref, cross1_ref, keep_ref), (own2_ref, cross2_ref, give_ref)):
        acc = lax.dot_general(own[...], p_own, TN, preferred_element_type=f32)
        out_ref[...] = acc + lax.dot_general(cross[...], p_cross, TN, preferred_element_type=f32)


def spread_kernel(in_ref, *refs):
    refs[-1][...] = jnp.broadcast_to(in_ref[...][None], refs[-1].shape)


def sum_kernel(mine_ref, g1_ref, g2_ref, g3_ref, after_ref, out_ref):
    out_ref[...] = mine_ref[...] + g1_ref[...].astype(f32) + g2_ref[...].astype(f32) + g3_ref[...].astype(f32)


def first_stage(parts):
    got = []
    for half, axis in ((0, "x"), (1, "z")):
        got.append([send(parts[4 * half + k], along(axis, k)) for k in (1, 2, 3)])
    return got


def second_stage(parts, got, rows, after):
    mids, sums = [], []
    for half in range(2):
        mids.append([])
        for j in range(4):
            cut = lambda v: lax.slice_in_dim(v, j * rows, (j + 1) * rows).astype(f32)
            total = cut(parts[4 * half])
            for r in got[half]:
                total = total + cut(r)
            mids[half].append(total)
    for half, axis in ((0, "z"), (1, "x")):
        rs = [send(mids[half][k].astype(bf16), along(axis, k)) for k in (1, 2, 3)]
        out = jax.ShapeDtypeStruct(mids[half][0].shape, f32)
        sums.append(kernel_call(sum_kernel, [out], [VMEM] * 4 + [ANY], mids[half][0], *rs, after[half])[0])
    return jnp.concatenate(sums, axis=1)


def own_sum_kernel(at_ref, got_ref, direct_ref, mirror_ref):
    chip = at_ref[0] * 4 + at_ref[1]
    wide = mirror_ref.shape[2]
    direct_ref[...] = jnp.zeros_like(direct_ref)
    mirror_ref[...] = jnp.zeros_like(mirror_ref)
    for k in range(9):
        total = jnp.sum(got_ref[:, :, k * wide : (k + 1) * wide].astype(f32), axis=0)
        to = lax.rem(chip + k, 16)
        direct_ref[:, pl.ds(pl.multiple_of(to * wide, wide), wide)] = total
        mirror_ref[pl.ds(to, 1)] = total.astype(bf16)[None]


def join_kernel(at_ref, direct_ref, held_ref, given_ref, out_ref):
    chip = at_ref[0] * 4 + at_ref[1]
    low = at_ref[2] == 0
    rows = held_ref.shape[0]
    for j in range(16):
        mine = held_ref[:, j * rows : (j + 1) * rows].astype(f32)
        other = given_ref[:, j * rows : (j + 1) * rows].astype(f32)
        both = jnp.concatenate([jnp.where(low, mine, other), jnp.where(low, other, mine)], axis=1)
        cols = slice(2 * j * rows, 2 * (j + 1) * rows)
        near = lax.rem(j - chip + 16, 16) <= 8
        out_ref[:, cols] = jnp.where(near, direct_ref[:, cols], both)


def on_device(grads, covariance, test_grads, inverse_factor):
    tokens, feats = grads.shape
    z, x, c = lax.axis_index("z"), lax.axis_index("x"), lax.axis_index("c")
    yl, h = lax.axis_index("yl"), lax.axis_index("yh")
    rows = feats // 32
    tests = test_grads.shape[0]
    at = jnp.stack([z, x, c * rows, h]).astype(jnp.int32)
    shape = jax.ShapeDtypeStruct
    gt = grads.T
    sib = send(gt, flip("c"))

    pick = lambda v: lax.dynamic_index_in_dim(v.reshape(16, 2, rows, tokens), c, 1, keepdims=False)
    mine = pick(gt).reshape(feats // 2, tokens)
    far1 = send(mine, flip("yh"))
    sib_mine = pick(sib).reshape(feats // 2, tokens)
    far2 = send(sib_mine, flip("yh"))
    (own,) = kernel_call(
        own_kernel,
        [shape((16, rows, 18 * rows), bf16)],
        [VMEM] * 4 + [ANY],
        mine, sib_mine, gt, sib, far1,
        flops=3 * 16 * rows * feats * tokens,
    )

    (slots,) = kernel_call(
        slots_kernel,
        [shape((16, rows, 4 * rows + tests), bf16)],
        [VMEM, VMEM],
        inverse_factor, test_grads.T,
    )
    slots = lax.all_to_all(slots, ("z", "x"), split_axis=0, concat_axis=0, tiled=True)
    (pt,) = kernel_call(
        functools.partial(factor_kernel, 4 * rows),
        [shape((4 * rows, tests), f32)],
        [VMEM, ANY, ANY],
        slots.reshape(16 * rows, -1), own, far1,
        flops=2 * 16 * rows * 4 * rows * tests,
    )
    pt = pt.reshape(2, 2, rows, tests)
    half = lambda i: lax.dynamic_index_in_dim(pt, i, 1, keepdims=False)
    pt = half(c) + send(half(1 - c), flip("c"))
    pt = (pt + send(pt, flip("yl"))).astype(bf16)
    own = lax.all_to_all(own, ("z", "x"), split_axis=0, concat_axis=0, tiled=True)
    direct, mirror = kernel_call(
        own_sum_kernel,
        [shape((rows, feats), f32), shape((16, rows, 2 * rows), bf16)],
        [SMEM, VMEM],
        at, own,
    )
    mirror = lax.all_to_all(mirror, ("z", "x"), split_axis=0, concat_axis=0, tiled=True)
    cross = gram(at, far1, far2, gt, sib, pt, direct)
    crossed = first_stage(cross)
    (pt,) = kernel_call(
        spread_kernel, [shape((16,) + pt.shape, bf16)], [VMEM] + [ANY] * 4, pt, *crossed[0][:2], *crossed[1][:2]
    )
    pt = lax.all_to_all(pt, ("z", "x"), split_axis=0, concat_axis=0, tiled=True)

    keep, give = kernel_call(
        scores_kernel,
        [shape((tokens, tests), f32)] * 2,
        [SMEM] + [VMEM] * 5,
        at, pt, mine, sib_mine, far1, far2,
        flops=8 * 16 * rows * tokens * tests,
    )
    scores = keep + send(give, flip("c"))

    mirror = mirror.reshape(16 * rows, 2 * rows).T
    held = lax.dynamic_slice_in_dim(mirror, c * rows, rows, 0)
    given = send(lax.dynamic_slice_in_dim(mirror, (1 - c) * rows, rows, 0), flip("c"))
    (own,) = kernel_call(
        join_kernel, [shape((rows, feats), f32)], [SMEM] + [VMEM] * 3, at, direct, held, given
    )

    cross = second_stage(cross, crossed, rows, (keep, own))
    ours, theirs = jnp.where(yl == h, own, cross), jnp.where(yl == h, cross, own)
    term = ours + send(theirs.astype(bf16), flip("yl")).astype(f32)
    covariance_out = 0.9 * covariance + term / (tokens * 64)
    return scores, covariance_out


def solution(mesh):
    grid = Mesh(mesh.devices.reshape(SIZES), AXES)
    return jax.shard_map(
        on_device,
        mesh=grid,
        in_specs=(P(DP, "yh"), P(DP, "yh"), P("yh", DP), P(DP, None)),
        out_specs=(P(DP, "yh"), P(DP, "yh")),
        check_vma=False,
    )
```

```python
import functools

import jax
import jax.numpy as jnp
import numpy as np
from jax import lax
from jax.experimental import pallas as pl
from jax.experimental.pallas import tpu as pltpu
from jax.sharding import Mesh
from jax.sharding import PartitionSpec as P

AXES = ("yl", "z", "x", "c", "yh")
SIZES = (2, 4, 4, 2, 2)
DP = ("yl", "z", "x", "c")
NT = (((1,), (1,)), ((), ()))
TN = (((0,), (0,)), ((), ()))
bf16, f32 = jnp.bfloat16, jnp.float32
VMEM = pl.BlockSpec(memory_space=pltpu.VMEM)
ANY = pl.BlockSpec(memory_space=pl.ANY)
SMEM = pl.BlockSpec(memory_space=pltpu.SMEM)


def send(value, move, only=None):
    pairs = []
    for i in range(int(np.prod(SIZES))):
        at = dict(zip(AXES, (int(v) for v in np.unravel_index(i, SIZES))))
        if only is None or only(at):
            to = {**at, **move(at)}
            pairs.append((i, int(np.ravel_multi_index([to[a] for a in AXES], SIZES))))
    return lax.ppermute(value, AXES, pairs)


def along(axis, k):
    return lambda at: {axis: (at[axis] + k) % 4}


def flip(*axes):
    return lambda at: {a: 1 - at[a] for a in axes}


def kernel_call(body, outs, specs, *args, flops=0):
    nbytes = sum(a.size * a.dtype.itemsize for a in args) + sum(o.size * o.dtype.itemsize for o in outs)
    return pl.pallas_call(
        body,
        out_shape=outs,
        in_specs=specs,
        out_specs=[VMEM] * len(outs),
        cost_estimate=pl.CostEstimate(flops=flops, bytes_accessed=nbytes, transcendentals=0),
    )(*args)


def slots_kernel(f_ref, t_ref, after_ref, out_ref):
    wide = f_ref.shape[1] // 32
    for s in range(16):
        out_ref[s, :, :wide] = f_ref[:, s * wide : (s + 1) * wide]
        out_ref[s, :, wide : 2 * wide] = f_ref[:, (16 + s) * wide : (17 + s) * wide]
        out_ref[s, :, 2 * wide :] = t_ref[...]


def factor_kernel(wide, slots_ref, after_ref, also_ref, out_ref):
    out_ref[...] = lax.dot_general(
        slots_ref[:, :wide], slots_ref[:, wide:], TN, preferred_element_type=f32
    )


def pick_kernel(at_ref, gt_ref, sib_ref, out_ref):
    for i, ref in enumerate((gt_ref, sib_ref)):
        for b in range(16):
            start = pl.ds(pl.multiple_of(b * 128 + at_ref[2], 64), 64)
            out_ref[(16 * i + b) * 64 : (16 * i + b + 1) * 64, :] = ref[start, :]


def gram_kernel(half, at_ref, a_ref, b1_ref, b2_ref, after_ref, *outs):
    z, x = at_ref[0], at_ref[1]
    rows, m, n, tile = 64, a_ref.shape[0] // 2, b1_ref.shape[0] // 2, 256
    left1, left2 = [], []
    for k in range(4):
        for j in range(4):
            dx, dz = (k, j) if half == 0 else (j, k)
            block = (lax.rem(z + dz, 4) * 4 + lax.rem(x + dx, 4)) * rows
            left1.append(a_ref[pl.ds(pl.multiple_of(block, rows), rows), :])
            left2.append(a_ref[pl.ds(pl.multiple_of(block + m, rows), rows), :])
    left1, left2 = jnp.concatenate(left1), jnp.concatenate(left2)
    for t in range(n // tile):
        cols = pl.ds(half * n + t * tile, tile)
        acc = lax.dot_general(left1, b1_ref[cols, :], NT, preferred_element_type=f32)
        acc += lax.dot_general(left2, b2_ref[cols, :], NT, preferred_element_type=f32)
        for k in range(4):
            outs[k][:, t * tile : (t + 1) * tile] = acc[4 * k * rows : 4 * (k + 1) * rows].astype(bf16)


def gram(half, at, a, b1, b2, after):
    n = b1.shape[0]
    return kernel_call(
        functools.partial(gram_kernel, half),
        [jax.ShapeDtypeStruct((256, n // 2), bf16)] * 4,
        [SMEM] + [VMEM] * 3 + [ANY],
        at, a, b1, b2, after,
        flops=a.shape[0] * n * b1.shape[1],
    )


def scores_kernel(at_ref, pt_ref, own_ref, cross_ref, keep_ref, give_ref):
    h = at_ref[3]
    m = own_ref.shape[0] // 2
    p_own = pt_ref[:, pl.ds(h, 1), :, :].reshape(m, pt_ref.shape[-1])
    p_cross = pt_ref[:, pl.ds(1 - h, 1), :, :].reshape(m, pt_ref.shape[-1])
    for side, out_ref in enumerate((keep_ref, give_ref)):
        s = slice(side * m, (side + 1) * m)
        acc = lax.dot_general(own_ref[s, :], p_own, TN, preferred_element_type=f32)
        out_ref[...] = acc + lax.dot_general(cross_ref[s, :], p_cross, TN, preferred_element_type=f32)


def sum_kernel(mine_ref, g1_ref, g2_ref, g3_ref, after_ref, out_ref):
    out_ref[...] = mine_ref[...] + g1_ref[...].astype(f32) + g2_ref[...].astype(f32) + g3_ref[...].astype(f32)


def first_stage(parts, rows, axis):
    got = [send(parts[k], along(axis, k)) for k in (1, 2, 3)]
    mids = []
    for j in range(4):
        cut = lambda v: lax.slice_in_dim(v, j * rows, (j + 1) * rows).astype(f32)
        mids.append(cut(parts[0]) + cut(got[0]) + cut(got[1]) + cut(got[2]))
    return mids


def second_stage(own, cross, axis, after):
    both = [jnp.concatenate([a, b]) for a, b in zip(own, cross)]
    got = [send(both[k].astype(bf16), along(axis, k)) for k in (1, 2, 3)]
    out = jax.ShapeDtypeStruct(both[0].shape, f32)
    return kernel_call(sum_kernel, [out], [VMEM] * 4 + [ANY], both[0], *got, after)[0]


def on_device(grads, covariance, test_grads, inverse_factor):
    tokens, feats = grads.shape
    z, x, c = lax.axis_index("z"), lax.axis_index("x"), lax.axis_index("c")
    yl, h = lax.axis_index("yl"), lax.axis_index("yh")
    rows = feats // 32
    tests = test_grads.shape[0]
    at = jnp.stack([z, x, c * rows, h]).astype(jnp.int32)
    shape = jax.ShapeDtypeStruct
    gt = grads.T
    sib = send(gt, flip("c"))

    (picked,) = kernel_call(pick_kernel, [shape((feats, tokens), bf16)], [SMEM, VMEM, VMEM], at, gt, sib)
    arrived = send(picked, flip("yh"))
    own = [gram(0, at, picked, gt, sib, picked)]
    own.append(gram(1, at, picked, gt, sib, own[0][0]))
    cross = [gram(0, at, arrived, gt, sib, own[1][0])]
    cross.append(gram(1, at, arrived, gt, sib, cross[0][0]))

    (slots,) = kernel_call(
        slots_kernel,
        [shape((16, rows, 4 * rows + tests), bf16)],
        [VMEM, VMEM, ANY],
        inverse_factor, test_grads.T, own[1][0],
    )
    slots = lax.all_to_all(slots, ("z", "x"), split_axis=0, concat_axis=0, tiled=True)
    (pt,) = kernel_call(
        functools.partial(factor_kernel, 4 * rows),
        [shape((4 * rows, tests), f32)],
        [VMEM, ANY, ANY],
        slots.reshape(16 * rows, -1), own[1][0], arrived,
        flops=2 * 16 * rows * 4 * rows * tests,
    )
    pt = pt.reshape(2, 2, rows, tests)
    half = lambda i: lax.dynamic_index_in_dim(pt, i, 1, keepdims=False)
    pt = half(c) + send(half(1 - c), flip("c"))
    pt = (pt + send(pt, flip("yl"))).astype(bf16)
    pt = jnp.broadcast_to(pt[None], (16,) + pt.shape)
    pt = lax.all_to_all(pt, ("z", "x"), split_axis=0, concat_axis=0, tiled=True)

    keep, give = kernel_call(
        scores_kernel,
        [shape((tokens, tests), f32)] * 2,
        [SMEM] + [VMEM] * 3,
        at, pt, picked, arrived,
        flops=8 * 16 * rows * tokens * tests,
    )
    scores = keep + send(give, flip("c"))

    sums = []
    for half, (first, second) in enumerate((("x", "z"), ("z", "x"))):
        mids = [first_stage(parts[half], rows, first) for parts in (own, cross)]
        sums.append(second_stage(*mids, second, keep))
    sums = jnp.concatenate(sums, axis=1)
    own, cross = sums[:rows], sums[rows:]
    ours, theirs = jnp.where(yl == h, own, cross), jnp.where(yl == h, cross, own)
    term = ours + send(theirs.astype(bf16), flip("yl")).astype(f32)
    covariance_out = 0.9 * covariance + term / (tokens * 64)
    return scores, covariance_out


def solution(mesh):
    grid = Mesh(mesh.devices.reshape(SIZES), AXES)
    return jax.shard_map(
        on_device,
        mesh=grid,
        in_specs=(P(DP, "yh"), P(DP, "yh"), P("yh", DP), P(DP, None)),
        out_specs=(P(DP, "yh"), P(DP, "yh")),
        check_vma=False,
    )
```

```python
import functools

import jax
import jax.numpy as jnp
import numpy as np
from jax import lax
from jax.experimental import pallas as pl
from jax.experimental.pallas import tpu as pltpu
from jax.sharding import Mesh
from jax.sharding import PartitionSpec as P

AXES = ("yl", "z", "x", "c", "yh")
SIZES = (2, 4, 4, 2, 2)
DP = ("yl", "z", "x", "c")
NT = (((1,), (1,)), ((), ()))
TN = (((0,), (0,)), ((), ()))
bf16, f32 = jnp.bfloat16, jnp.float32
VMEM = pl.BlockSpec(memory_space=pltpu.VMEM)
ANY = pl.BlockSpec(memory_space=pl.ANY)
SMEM = pl.BlockSpec(memory_space=pltpu.SMEM)


def send(value, move, only=None):
    pairs = []
    for i in range(int(np.prod(SIZES))):
        at = dict(zip(AXES, (int(v) for v in np.unravel_index(i, SIZES))))
        if only is None or only(at):
            to = {**at, **move(at)}
            pairs.append((i, int(np.ravel_multi_index([to[a] for a in AXES], SIZES))))
    return lax.ppermute(value, AXES, pairs)


def along(axis, k):
    return lambda at: {axis: (at[axis] + k) % 4}


def flip(*axes):
    return lambda at: {a: 1 - at[a] for a in axes}


def kernel_call(body, outs, specs, *args, flops=0):
    nbytes = sum(a.size * a.dtype.itemsize for a in args) + sum(o.size * o.dtype.itemsize for o in outs)
    return pl.pallas_call(
        body,
        out_shape=outs,
        in_specs=specs,
        out_specs=[VMEM] * len(outs),
        cost_estimate=pl.CostEstimate(flops=flops, bytes_accessed=nbytes, transcendentals=0),
    )(*args)


def slots_kernel(f_ref, t_ref, out_ref):
    wide = f_ref.shape[1] // 32
    for s in range(16):
        out_ref[s, :, :wide] = f_ref[:, s * wide : (s + 1) * wide]
        out_ref[s, :, wide : 2 * wide] = f_ref[:, (16 + s) * wide : (17 + s) * wide]
        out_ref[s, :, 2 * wide :] = t_ref[...]


def factor_kernel(wide, slots_ref, after_ref, also_ref, out_ref):
    out_ref[...] = lax.dot_general(
        slots_ref[:, :wide], slots_ref[:, wide:], TN, preferred_element_type=f32
    )


def pick_kernel(at_ref, gt_ref, sib_ref, out_ref):
    for i, ref in enumerate((gt_ref, sib_ref)):
        for b in range(16):
            start = pl.ds(pl.multiple_of(b * 128 + at_ref[2], 64), 64)
            out_ref[(16 * i + b) * 64 : (16 * i + b + 1) * 64, :] = ref[start, :]


def own_kernel(a_ref, b1_ref, b2_ref, out_ref):
    rows = out_ref.shape[1]
    wide = 2 * rows
    for g in range(4):
        left1 = a_ref[4 * g * rows : 4 * (g + 1) * rows, :]
        left2 = a_ref[(16 + 4 * g) * rows : (20 + 4 * g) * rows, :]
        for q in range(3):
            cols = pl.ds((g + q) % 4 * 4 * wide, 4 * wide)
            acc = lax.dot_general(left1, b1_ref[cols, :], NT, preferred_element_type=f32)
            acc += lax.dot_general(left2, b2_ref[cols, :], NT, preferred_element_type=f32)
            acc = acc.astype(bf16)
            for i in range(4):
                lo, hi = max(4 * q, i), min(4 * q + 4, i + 9)
                if lo < hi:
                    piece = acc[i * rows : (i + 1) * rows, (lo - 4 * q) * wide : (hi - 4 * q) * wide]
                    out_ref[4 * g + i, :, (lo - i) * wide : (hi - i) * wide] = piece


def gram_kernel(at_ref, a_ref, b1_ref, b2_ref, after_ref, *outs):
    z, x = at_ref[0], at_ref[1]
    rows, m, n, tile = 64, a_ref.shape[0] // 2, b1_ref.shape[0] // 2, 256
    for half in range(2):
        left1, left2 = [], []
        for k in range(4):
            for j in range(4):
                dx, dz = (k, j) if half == 0 else (j, k)
                block = (lax.rem(z + dz, 4) * 4 + lax.rem(x + dx, 4)) * rows
                left1.append(a_ref[pl.ds(pl.multiple_of(block, rows), rows), :])
                left2.append(a_ref[pl.ds(pl.multiple_of(block + m, rows), rows), :])
        left1, left2 = jnp.concatenate(left1), jnp.concatenate(left2)
        for t in range(n // tile):
            cols = pl.ds(half * n + t * tile, tile)
            acc = lax.dot_general(left1, b1_ref[cols, :], NT, preferred_element_type=f32)
            acc += lax.dot_general(left2, b2_ref[cols, :], NT, preferred_element_type=f32)
            for k in range(4):
                part = acc[4 * k * rows : 4 * (k + 1) * rows].astype(bf16)
                outs[4 * half + k][:, t * tile : (t + 1) * tile] = part


def gram(at, a, b1, b2, after):
    n = b1.shape[0]
    return kernel_call(
        gram_kernel,
        [jax.ShapeDtypeStruct((256, n // 2), bf16)] * 8,
        [SMEM] + [VMEM] * 3 + [ANY],
        at, a, b1, b2, after,
        flops=2 * a.shape[0] * n * b1.shape[1],
    )


def scores_kernel(at_ref, pt_ref, own_ref, cross_ref, keep_ref, give_ref):
    h = at_ref[3]
    m = own_ref.shape[0] // 2
    p_own = pt_ref[:, pl.ds(h, 1), :, :].reshape(m, pt_ref.shape[-1])
    p_cross = pt_ref[:, pl.ds(1 - h, 1), :, :].reshape(m, pt_ref.shape[-1])
    for side, out_ref in enumerate((keep_ref, give_ref)):
        s = slice(side * m, (side + 1) * m)
        acc = lax.dot_general(own_ref[s, :], p_own, TN, preferred_element_type=f32)
        out_ref[...] = acc + lax.dot_general(cross_ref[s, :], p_cross, TN, preferred_element_type=f32)


def scatter_sum(parts, rows):
    got, mids, sums = [], [], []
    for half, axis in ((0, "x"), (1, "z")):
        got.append([send(parts[4 * half + k], along(axis, k)) for k in (1, 2, 3)])
    for half in range(2):
        mids.append([])
        for j in range(4):
            cut = lambda v: lax.slice_in_dim(v, j * rows, (j + 1) * rows).astype(f32)
            total = cut(parts[4 * half])
            for r in got[half]:
                total = total + cut(r)
            mids[half].append(total)
    for half, axis in ((0, "z"), (1, "x")):
        rs = [send(mids[half][k].astype(bf16), along(axis, k)) for k in (1, 2, 3)]
        sums.append(mids[half][0] + rs[0].astype(f32) + rs[1].astype(f32) + rs[2].astype(f32))
    return jnp.concatenate(sums, axis=1)


def own_sum_kernel(at_ref, got_ref, direct_ref, mirror_ref):
    chip = at_ref[0] * 4 + at_ref[1]
    wide = mirror_ref.shape[2]
    direct_ref[...] = jnp.zeros_like(direct_ref)
    mirror_ref[...] = jnp.zeros_like(mirror_ref)
    for k in range(9):
        total = jnp.sum(got_ref[:, :, k * wide : (k + 1) * wide].astype(f32), axis=0)
        to = lax.rem(chip + k, 16)
        direct_ref[:, pl.ds(pl.multiple_of(to * wide, wide), wide)] = total
        mirror_ref[pl.ds(to, 1)] = total.astype(bf16)[None]


def join_kernel(at_ref, direct_ref, held_ref, given_ref, out_ref):
    chip = at_ref[0] * 4 + at_ref[1]
    low = at_ref[2] == 0
    rows = held_ref.shape[0]
    for j in range(16):
        mine = held_ref[:, j * rows : (j + 1) * rows].astype(f32)
        other = given_ref[:, j * rows : (j + 1) * rows].astype(f32)
        both = jnp.concatenate([jnp.where(low, mine, other), jnp.where(low, other, mine)], axis=1)
        cols = slice(2 * j * rows, 2 * (j + 1) * rows)
        near = lax.rem(j - chip + 16, 16) <= 8
        out_ref[:, cols] = jnp.where(near, direct_ref[:, cols], both)


def on_device(grads, covariance, test_grads, inverse_factor):
    tokens, feats = grads.shape
    z, x, c = lax.axis_index("z"), lax.axis_index("x"), lax.axis_index("c")
    yl, h = lax.axis_index("yl"), lax.axis_index("yh")
    rows = feats // 32
    tests = test_grads.shape[0]
    at = jnp.stack([z, x, c * rows, h]).astype(jnp.int32)
    shape = jax.ShapeDtypeStruct
    gt = grads.T
    sib = send(gt, flip("c"))

    (picked,) = kernel_call(pick_kernel, [shape((feats, tokens), bf16)], [SMEM, VMEM, VMEM], at, gt, sib)
    arrived = send(picked, flip("yh"))
    (own,) = kernel_call(
        own_kernel,
        [shape((16, rows, 18 * rows), bf16)],
        [VMEM] * 3,
        picked, gt, sib,
        flops=3 * 16 * rows * feats * tokens,
    )
    cross = gram(at, arrived, gt, sib, own)

    (slots,) = kernel_call(
        slots_kernel,
        [shape((16, rows, 4 * rows + tests), bf16)],
        [VMEM, VMEM],
        inverse_factor, test_grads.T,
    )
    slots = lax.all_to_all(slots, ("z", "x"), split_axis=0, concat_axis=0, tiled=True)
    (pt,) = kernel_call(
        functools.partial(factor_kernel, 4 * rows),
        [shape((4 * rows, tests), f32)],
        [VMEM, ANY, ANY],
        slots.reshape(16 * rows, -1), own, arrived,
        flops=2 * 16 * rows * 4 * rows * tests,
    )
    pt = pt.reshape(2, 2, rows, tests)
    half = lambda i: lax.dynamic_index_in_dim(pt, i, 1, keepdims=False)
    pt = half(c) + send(half(1 - c), flip("c"))
    pt = (pt + send(pt, flip("yl"))).astype(bf16)
    pt = jnp.broadcast_to(pt[None], (16,) + pt.shape)
    pt = lax.all_to_all(pt, ("z", "x"), split_axis=0, concat_axis=0, tiled=True)

    keep, give = kernel_call(
        scores_kernel,
        [shape((tokens, tests), f32)] * 2,
        [SMEM] + [VMEM] * 3,
        at, pt, picked, arrived,
        flops=8 * 16 * rows * tokens * tests,
    )
    scores = keep + send(give, flip("c"))

    own = lax.all_to_all(own, ("z", "x"), split_axis=0, concat_axis=0, tiled=True)
    direct, mirror = kernel_call(
        own_sum_kernel,
        [shape((rows, feats), f32), shape((16, rows, 2 * rows), bf16)],
        [SMEM, VMEM],
        at, own,
    )
    mirror = lax.all_to_all(mirror, ("z", "x"), split_axis=0, concat_axis=0, tiled=True)
    mirror = mirror.reshape(16 * rows, 2 * rows).T
    held = lax.dynamic_slice_in_dim(mirror, c * rows, rows, 0)
    given = send(lax.dynamic_slice_in_dim(mirror, (1 - c) * rows, rows, 0), flip("c"))
    (own,) = kernel_call(
        join_kernel, [shape((rows, feats), f32)], [SMEM] + [VMEM] * 3, at, direct, held, given
    )

    cross = scatter_sum(cross, rows)
    ours, theirs = jnp.where(yl == h, own, cross), jnp.where(yl == h, cross, own)
    term = ours + send(theirs.astype(bf16), flip("yl")).astype(f32)
    covariance_out = 0.9 * covariance + term / (tokens * 64)
    return scores, covariance_out


def solution(mesh):
    grid = Mesh(mesh.devices.reshape(SIZES), AXES)
    return jax.shard_map(
        on_device,
        mesh=grid,
        in_specs=(P(DP, "yh"), P(DP, "yh"), P("yh", DP), P(DP, None)),
        out_specs=(P(DP, "yh"), P(DP, "yh")),
        check_vma=False,
    )
```

```python
import functools

import jax
import jax.numpy as jnp
import numpy as np
from jax import lax
from jax.experimental import pallas as pl
from jax.experimental.pallas import tpu as pltpu
from jax.sharding import Mesh
from jax.sharding import PartitionSpec as P

AXES = ("yl", "z", "x", "c", "yh")
SIZES = (2, 4, 4, 2, 2)
DP = ("yl", "z", "x", "c")
NT = (((1,), (1,)), ((), ()))
TN = (((0,), (0,)), ((), ()))
bf16, f32 = jnp.bfloat16, jnp.float32
VMEM = pl.BlockSpec(memory_space=pltpu.VMEM)
ANY = pl.BlockSpec(memory_space=pl.ANY)
SMEM = pl.BlockSpec(memory_space=pltpu.SMEM)


def send(value, move, only=None):
    pairs = []
    for i in range(int(np.prod(SIZES))):
        at = dict(zip(AXES, (int(v) for v in np.unravel_index(i, SIZES))))
        if only is None or only(at):
            to = {**at, **move(at)}
            pairs.append((i, int(np.ravel_multi_index([to[a] for a in AXES], SIZES))))
    return lax.ppermute(value, AXES, pairs)


def along(axis, k):
    return lambda at: {axis: (at[axis] + k) % 4}


def flip(*axes):
    return lambda at: {a: 1 - at[a] for a in axes}


def kernel_call(body, outs, specs, *args, flops=0):
    nbytes = sum(a.size * a.dtype.itemsize for a in args) + sum(o.size * o.dtype.itemsize for o in outs)
    return pl.pallas_call(
        body,
        out_shape=outs,
        in_specs=specs,
        out_specs=[VMEM] * len(outs),
        cost_estimate=pl.CostEstimate(flops=flops, bytes_accessed=nbytes, transcendentals=0),
    )(*args)


def slots_kernel(f_ref, t_ref, out_ref):
    wide = f_ref.shape[1] // 32
    for s in range(16):
        out_ref[s, :, :wide] = f_ref[:, s * wide : (s + 1) * wide]
        out_ref[s, :, wide : 2 * wide] = f_ref[:, (16 + s) * wide : (17 + s) * wide]
        out_ref[s, :, 2 * wide :] = t_ref[...]


def factor_kernel(wide, slots_ref, after_ref, also_ref, out_ref):
    out_ref[...] = lax.dot_general(
        slots_ref[:, :wide], slots_ref[:, wide:], TN, preferred_element_type=f32
    )


def pick_kernel(at_ref, gt_ref, sib_ref, out_ref):
    for i, ref in enumerate((gt_ref, sib_ref)):
        for b in range(16):
            start = pl.ds(pl.multiple_of(b * 128 + at_ref[2], 64), 64)
            out_ref[(16 * i + b) * 64 : (16 * i + b + 1) * 64, :] = ref[start, :]


def own_kernel(a_ref, b1_ref, b2_ref, out_ref):
    rows = out_ref.shape[1]
    wide = 2 * rows
    for g in range(4):
        left1 = a_ref[4 * g * rows : 4 * (g + 1) * rows, :]
        left2 = a_ref[(16 + 4 * g) * rows : (20 + 4 * g) * rows, :]
        for q in range(3):
            cols = pl.ds((g + q) % 4 * 4 * wide, 4 * wide)
            acc = lax.dot_general(left1, b1_ref[cols, :], NT, preferred_element_type=f32)
            acc += lax.dot_general(left2, b2_ref[cols, :], NT, preferred_element_type=f32)
            acc = acc.astype(bf16)
            for i in range(4):
                lo, hi = max(4 * q, i), min(4 * q + 4, i + 9)
                if lo < hi:
                    piece = acc[i * rows : (i + 1) * rows, (lo - 4 * q) * wide : (hi - 4 * q) * wide]
                    out_ref[4 * g + i, :, (lo - i) * wide : (hi - i) * wide] = piece


def gram_kernel(at_ref, a_ref, b1_ref, b2_ref, after_ref, *outs):
    z, x = at_ref[0], at_ref[1]
    rows, m, n, tile = 64, a_ref.shape[0] // 2, b1_ref.shape[0] // 2, 256
    for half in range(2):
        left1, left2 = [], []
        for k in range(4):
            for j in range(4):
                dx, dz = (k, j) if half == 0 else (j, k)
                block = (lax.rem(z + dz, 4) * 4 + lax.rem(x + dx, 4)) * rows
                left1.append(a_ref[pl.ds(pl.multiple_of(block, rows), rows), :])
                left2.append(a_ref[pl.ds(pl.multiple_of(block + m, rows), rows), :])
        left1, left2 = jnp.concatenate(left1), jnp.concatenate(left2)
        for t in range(n // tile):
            cols = pl.ds(half * n + t * tile, tile)
            acc = lax.dot_general(left1, b1_ref[cols, :], NT, preferred_element_type=f32)
            acc += lax.dot_general(left2, b2_ref[cols, :], NT, preferred_element_type=f32)
            for k in range(4):
                part = acc[4 * k * rows : 4 * (k + 1) * rows].astype(bf16)
                outs[4 * half + k][:, t * tile : (t + 1) * tile] = part


def gram(at, a, b1, b2, after):
    n = b1.shape[0]
    return kernel_call(
        gram_kernel,
        [jax.ShapeDtypeStruct((256, n // 2), bf16)] * 8,
        [SMEM] + [VMEM] * 3 + [ANY],
        at, a, b1, b2, after,
        flops=2 * a.shape[0] * n * b1.shape[1],
    )


def scores_kernel(at_ref, pt_ref, own_ref, cross_ref, keep_ref, give_ref):
    h = at_ref[3]
    m = own_ref.shape[0] // 2
    p_own = pt_ref[:, pl.ds(pl.multiple_of(h * 64, 64), 64), :].reshape(m, pt_ref.shape[-1])
    p_cross = pt_ref[:, pl.ds(pl.multiple_of((1 - h) * 64, 64), 64), :].reshape(m, pt_ref.shape[-1])
    for side, out_ref in enumerate((keep_ref, give_ref)):
        s = slice(side * m, (side + 1) * m)
        acc = lax.dot_general(own_ref[s, :], p_own, TN, preferred_element_type=f32)
        out_ref[...] = acc + lax.dot_general(cross_ref[s, :], p_cross, TN, preferred_element_type=f32)


def first_stage(parts):
    got = []
    for half, axis in ((0, "x"), (1, "z")):
        got.append([send(parts[4 * half + k], along(axis, k)) for k in (1, 2, 3)])
    return got


def second_stage(parts, got, rows):
    sums = []
    for half, axis in ((0, "z"), (1, "x")):
        mids = []
        for j in range(4):
            cut = lambda v: lax.slice_in_dim(v, j * rows, (j + 1) * rows).astype(f32)
            total = cut(parts[4 * half])
            for r in got[half]:
                total = total + cut(r)
            mids.append(total)
        rs = [send(mids[k].astype(bf16), along(axis, k)) for k in (1, 2, 3)]
        sums.append(mids[0] + rs[0].astype(f32) + rs[1].astype(f32) + rs[2].astype(f32))
    return jnp.concatenate(sums, axis=1)


def own_sum_kernel(at_ref, got_ref, pt_ref, after_ref, also_ref, direct_ref, slots_ref):
    chip = at_ref[0] * 4 + at_ref[1]
    rows = direct_ref.shape[0]
    wide, low = 2 * rows, rows // 2
    direct_ref[...] = jnp.zeros_like(direct_ref)
    slots_ref[:, :wide, :] = jnp.broadcast_to(pt_ref[...][None], (16, wide, pt_ref.shape[1]))
    slots_ref[:, wide:, :] = jnp.zeros_like(slots_ref[:, wide:, :])
    for k in range(9):
        total = jnp.sum(got_ref[:, :, k * wide : (k + 1) * wide].astype(f32), axis=0)
        to = lax.rem(chip + k, 16)
        direct_ref[:, pl.ds(pl.multiple_of(to * wide, wide), wide)] = total
        both = jnp.concatenate([total[:low], total[low:]], axis=1).astype(bf16)
        slots_ref[pl.ds(to, 1), wide:, :] = both[None]


def join_kernel(at_ref, direct_ref, held_ref, given_ref, out_ref):
    chip = at_ref[0] * 4 + at_ref[1]
    low = at_ref[2] == 0
    rows = held_ref.shape[0]
    for j in range(16):
        mine = held_ref[:, j * rows : (j + 1) * rows].astype(f32)
        other = given_ref[:, j * rows : (j + 1) * rows].astype(f32)
        both = jnp.concatenate([jnp.where(low, mine, other), jnp.where(low, other, mine)], axis=1)
        cols = slice(2 * j * rows, 2 * (j + 1) * rows)
        near = lax.rem(j - chip + 16, 16) <= 8
        out_ref[:, cols] = jnp.where(near, direct_ref[:, cols], both)


def on_device(grads, covariance, test_grads, inverse_factor):
    tokens, feats = grads.shape
    z, x, c = lax.axis_index("z"), lax.axis_index("x"), lax.axis_index("c")
    yl, h = lax.axis_index("yl"), lax.axis_index("yh")
    rows = feats // 32
    tests = test_grads.shape[0]
    at = jnp.stack([z, x, c * rows, h]).astype(jnp.int32)
    shape = jax.ShapeDtypeStruct
    gt = grads.T
    sib = send(gt, flip("c"))

    (picked,) = kernel_call(pick_kernel, [shape((feats, tokens), bf16)], [SMEM, VMEM, VMEM], at, gt, sib)
    arrived = send(picked, flip("yh"))
    (own,) = kernel_call(
        own_kernel,
        [shape((16, rows, 18 * rows), bf16)],
        [VMEM] * 3,
        picked, gt, sib,
        flops=3 * 16 * rows * feats * tokens,
    )
    cross = gram(at, arrived, gt, sib, own)
    crossed = first_stage(cross)

    (slots,) = kernel_call(
        slots_kernel,
        [shape((16, rows, 4 * rows + tests), bf16)],
        [VMEM, VMEM],
        inverse_factor, test_grads.T,
    )
    slots = lax.all_to_all(slots, ("z", "x"), split_axis=0, concat_axis=0, tiled=True)
    (pt,) = kernel_call(
        functools.partial(factor_kernel, 4 * rows),
        [shape((4 * rows, tests), f32)],
        [VMEM, ANY, ANY],
        slots.reshape(16 * rows, -1), own, cross[0],
        flops=2 * 16 * rows * 4 * rows * tests,
    )
    pt = pt.reshape(2, 2, rows, tests)
    half = lambda i: lax.dynamic_index_in_dim(pt, i, 1, keepdims=False)
    pt = half(c) + send(half(1 - c), flip("c"))
    pt = (pt + send(pt, flip("yl"))).astype(bf16)

    own = lax.all_to_all(own, ("z", "x"), split_axis=0, concat_axis=0, tiled=True)
    direct, slots = kernel_call(
        own_sum_kernel,
        [shape((rows, feats), f32), shape((16, 2 * rows + rows // 2, tests), bf16)],
        [SMEM, VMEM, VMEM, ANY, ANY],
        at, own, pt.reshape(2 * rows, tests), crossed[0][0], crossed[1][0],
    )
    slots = lax.all_to_all(slots, ("z", "x"), split_axis=0, concat_axis=0, tiled=True)
    mirror = slots[:, 2 * rows :]
    mirror = jnp.concatenate([mirror[..., : 2 * rows], mirror[..., 2 * rows :]], axis=1)

    keep, give = kernel_call(
        scores_kernel,
        [shape((tokens, tests), f32)] * 2,
        [SMEM] + [VMEM] * 3,
        at, slots, picked, arrived,
        flops=8 * 16 * rows * tokens * tests,
    )
    scores = keep + send(give, flip("c"))

    mirror = mirror.reshape(16 * rows, 2 * rows).T
    held = lax.dynamic_slice_in_dim(mirror, c * rows, rows, 0)
    given = send(lax.dynamic_slice_in_dim(mirror, (1 - c) * rows, rows, 0), flip("c"))
    (own,) = kernel_call(
        join_kernel, [shape((rows, feats), f32)], [SMEM] + [VMEM] * 3, at, direct, held, given
    )

    cross = second_stage(cross, crossed, rows)
    ours, theirs = jnp.where(yl == h, own, cross), jnp.where(yl == h, cross, own)
    term = ours + send(theirs.astype(bf16), flip("yl")).astype(f32)
    covariance_out = 0.9 * covariance + term / (tokens * 64)
    return scores, covariance_out


def solution(mesh):
    grid = Mesh(mesh.devices.reshape(SIZES), AXES)
    return jax.shard_map(
        on_device,
        mesh=grid,
        in_specs=(P(DP, "yh"), P(DP, "yh"), P("yh", DP), P(DP, None)),
        out_specs=(P(DP, "yh"), P(DP, "yh")),
        check_vma=False,
    )
```

```python
import functools

import jax
import jax.numpy as jnp
import numpy as np
from jax import lax
from jax.experimental import pallas as pl
from jax.experimental.pallas import tpu as pltpu
from jax.sharding import Mesh
from jax.sharding import PartitionSpec as P

AXES = ("yl", "z", "x", "c", "yh")
SIZES = (2, 4, 4, 2, 2)
DP = ("yl", "z", "x", "c")
NT = (((1,), (1,)), ((), ()))
TN = (((0,), (0,)), ((), ()))
bf16, f32 = jnp.bfloat16, jnp.float32
VMEM = pl.BlockSpec(memory_space=pltpu.VMEM)
ANY = pl.BlockSpec(memory_space=pl.ANY)
SMEM = pl.BlockSpec(memory_space=pltpu.SMEM)


def send(value, move, only=None):
    pairs = []
    for i in range(int(np.prod(SIZES))):
        at = dict(zip(AXES, (int(v) for v in np.unravel_index(i, SIZES))))
        if only is None or only(at):
            to = {**at, **move(at)}
            pairs.append((i, int(np.ravel_multi_index([to[a] for a in AXES], SIZES))))
    return lax.ppermute(value, AXES, pairs)


def along(axis, k):
    return lambda at: {axis: (at[axis] + k) % 4}


def flip(*axes):
    return lambda at: {a: 1 - at[a] for a in axes}


def kernel_call(body, outs, specs, *args, flops=0):
    nbytes = sum(a.size * a.dtype.itemsize for a in args) + sum(o.size * o.dtype.itemsize for o in outs)
    return pl.pallas_call(
        body,
        out_shape=outs,
        in_specs=specs,
        out_specs=[VMEM] * len(outs),
        cost_estimate=pl.CostEstimate(flops=flops, bytes_accessed=nbytes, transcendentals=0),
    )(*args)


def slots_kernel(f_ref, t_ref, out_ref):
    wide = f_ref.shape[1] // 32
    for s in range(16):
        out_ref[s, :, :wide] = f_ref[:, s * wide : (s + 1) * wide]
        out_ref[s, :, wide : 2 * wide] = f_ref[:, (16 + s) * wide : (17 + s) * wide]
        out_ref[s, :, 2 * wide :] = t_ref[...]


def factor_kernel(wide, slots_ref, after_ref, also_ref, out_ref):
    out_ref[...] = lax.dot_general(
        slots_ref[:, :wide], slots_ref[:, wide:], TN, preferred_element_type=f32
    )


def pick_kernel(at_ref, gt_ref, sib_ref, out_ref):
    for i, ref in enumerate((gt_ref, sib_ref)):
        for b in range(16):
            start = pl.ds(pl.multiple_of(b * 128 + at_ref[2], 64), 64)
            out_ref[(16 * i + b) * 64 : (16 * i + b + 1) * 64, :] = ref[start, :]


def own_kernel(a_ref, b1_ref, b2_ref, out_ref):
    rows = out_ref.shape[1]
    wide = 2 * rows
    for g in range(4):
        left1 = a_ref[4 * g * rows : 4 * (g + 1) * rows, :]
        left2 = a_ref[(16 + 4 * g) * rows : (20 + 4 * g) * rows, :]
        for q in range(3):
            cols = pl.ds((g + q) % 4 * 4 * wide, 4 * wide)
            acc = lax.dot_general(left1, b1_ref[cols, :], NT, preferred_element_type=f32)
            acc += lax.dot_general(left2, b2_ref[cols, :], NT, preferred_element_type=f32)
            acc = acc.astype(bf16)
            for i in range(4):
                lo, hi = max(4 * q, i), min(4 * q + 4, i + 9)
                if lo < hi:
                    piece = acc[i * rows : (i + 1) * rows, (lo - 4 * q) * wide : (hi - 4 * q) * wide]
                    out_ref[4 * g + i, :, (lo - i) * wide : (hi - i) * wide] = piece


def gram_kernel(at_ref, a_ref, b1_ref, b2_ref, after_ref, *outs):
    z, x = at_ref[0], at_ref[1]
    rows, m, n, tile = 64, a_ref.shape[0] // 2, b1_ref.shape[0] // 2, 256
    for half in range(2):
        left1, left2 = [], []
        for k in range(4):
            for j in range(4):
                dx, dz = (k, j) if half == 0 else (j, k)
                block = (lax.rem(z + dz, 4) * 4 + lax.rem(x + dx, 4)) * rows
                left1.append(a_ref[pl.ds(pl.multiple_of(block, rows), rows), :])
                left2.append(a_ref[pl.ds(pl.multiple_of(block + m, rows), rows), :])
        left1, left2 = jnp.concatenate(left1), jnp.concatenate(left2)
        for t in range(n // tile):
            cols = pl.ds(half * n + t * tile, tile)
            acc = lax.dot_general(left1, b1_ref[cols, :], NT, preferred_element_type=f32)
            acc += lax.dot_general(left2, b2_ref[cols, :], NT, preferred_element_type=f32)
            for k in range(4):
                part = acc[4 * k * rows : 4 * (k + 1) * rows].astype(bf16)
                outs[4 * half + k][:, t * tile : (t + 1) * tile] = part


def gram(at, a, b1, b2, after):
    n = b1.shape[0]
    return kernel_call(
        gram_kernel,
        [jax.ShapeDtypeStruct((256, n // 2), bf16)] * 8,
        [SMEM] + [VMEM] * 3 + [ANY],
        at, a, b1, b2, after,
        flops=2 * a.shape[0] * n * b1.shape[1],
    )


def scores_kernel(at_ref, pt_ref, own_ref, cross_ref, keep_ref, give_ref):
    h = at_ref[3]
    m = own_ref.shape[0] // 2
    p_own = pt_ref[:, pl.ds(pl.multiple_of(h * 64, 64), 64), :].reshape(m, pt_ref.shape[-1])
    p_cross = pt_ref[:, pl.ds(pl.multiple_of((1 - h) * 64, 64), 64), :].reshape(m, pt_ref.shape[-1])
    for side, out_ref in enumerate((keep_ref, give_ref)):
        s = slice(side * m, (side + 1) * m)
        acc = lax.dot_general(own_ref[s, :], p_own, TN, preferred_element_type=f32)
        out_ref[...] = acc + lax.dot_general(cross_ref[s, :], p_cross, TN, preferred_element_type=f32)


def first_stage(parts):
    got = []
    for half, axis in ((0, "x"), (1, "z")):
        got.append([send(parts[4 * half + k], along(axis, k)) for k in (1, 2, 3)])
    return got


def second_stage(parts, got, rows):
    sums = []
    for half, axis in ((0, "z"), (1, "x")):
        mids = []
        for j in range(4):
            cut = lambda v: lax.slice_in_dim(v, j * rows, (j + 1) * rows).astype(f32)
            total = cut(parts[4 * half])
            for r in got[half]:
                total = total + cut(r)
            mids.append(total)
        rs = [send(mids[k].astype(bf16), along(axis, k)) for k in (1, 2, 3)]
        sums.append(mids[0] + rs[0].astype(f32) + rs[1].astype(f32) + rs[2].astype(f32))
    return jnp.concatenate(sums, axis=1)


def own_sum_kernel(at_ref, got_ref, pt_ref, *refs):
    direct_ref, slots_ref = refs[-2:]
    chip = at_ref[0] * 4 + at_ref[1]
    rows = direct_ref.shape[0]
    wide, low = 2 * rows, rows // 2
    direct_ref[...] = jnp.zeros_like(direct_ref)
    slots_ref[:, :wide, :] = jnp.broadcast_to(pt_ref[...][None], (16, wide, pt_ref.shape[1]))
    slots_ref[:, wide:, :] = jnp.zeros_like(slots_ref[:, wide:, :])
    for k in range(9):
        total = jnp.sum(got_ref[:, :, k * wide : (k + 1) * wide].astype(f32), axis=0)
        to = lax.rem(chip + k, 16)
        direct_ref[:, pl.ds(pl.multiple_of(to * wide, wide), wide)] = total
        both = jnp.concatenate([total[:low], total[low:]], axis=1).astype(bf16)
        slots_ref[pl.ds(to, 1), wide:, :] = both[None]


def join_kernel(at_ref, direct_ref, held_ref, given_ref, out_ref):
    chip = at_ref[0] * 4 + at_ref[1]
    low = at_ref[2] == 0
    rows = held_ref.shape[0]
    for j in range(16):
        mine = held_ref[:, j * rows : (j + 1) * rows].astype(f32)
        other = given_ref[:, j * rows : (j + 1) * rows].astype(f32)
        both = jnp.concatenate([jnp.where(low, mine, other), jnp.where(low, other, mine)], axis=1)
        cols = slice(2 * j * rows, 2 * (j + 1) * rows)
        near = lax.rem(j - chip + 16, 16) <= 8
        out_ref[:, cols] = jnp.where(near, direct_ref[:, cols], both)


def on_device(grads, covariance, test_grads, inverse_factor):
    tokens, feats = grads.shape
    z, x, c = lax.axis_index("z"), lax.axis_index("x"), lax.axis_index("c")
    yl, h = lax.axis_index("yl"), lax.axis_index("yh")
    rows = feats // 32
    tests = test_grads.shape[0]
    at = jnp.stack([z, x, c * rows, h]).astype(jnp.int32)
    shape = jax.ShapeDtypeStruct
    gt = grads.T
    sib = send(gt, flip("c"))

    (picked,) = kernel_call(pick_kernel, [shape((feats, tokens), bf16)], [SMEM, VMEM, VMEM], at, gt, sib)
    arrived = send(picked, flip("yh"))
    (own,) = kernel_call(
        own_kernel,
        [shape((16, rows, 18 * rows), bf16)],
        [VMEM] * 3,
        picked, gt, sib,
        flops=3 * 16 * rows * feats * tokens,
    )
    cross = gram(at, arrived, gt, sib, own)
    crossed = first_stage(cross)

    (slots,) = kernel_call(
        slots_kernel,
        [shape((16, rows, 4 * rows + tests), bf16)],
        [VMEM, VMEM],
        inverse_factor, test_grads.T,
    )
    slots = lax.all_to_all(slots, ("z", "x"), split_axis=0, concat_axis=0, tiled=True)
    (pt,) = kernel_call(
        functools.partial(factor_kernel, 4 * rows),
        [shape((4 * rows, tests), f32)],
        [VMEM, ANY, ANY],
        slots.reshape(16 * rows, -1), own, cross[0],
        flops=2 * 16 * rows * 4 * rows * tests,
    )
    pt = pt.reshape(2, 2, rows, tests)
    half = lambda i: lax.dynamic_index_in_dim(pt, i, 1, keepdims=False)
    pt = half(c) + send(half(1 - c), flip("c"))
    pt = (pt + send(pt, flip("yl"))).astype(bf16)

    own = lax.all_to_all(own, ("z", "x"), split_axis=0, concat_axis=0, tiled=True)
    direct, slots = kernel_call(
        own_sum_kernel,
        [shape((rows, feats), f32), shape((16, 2 * rows + rows // 2, tests), bf16)],
        [SMEM, VMEM, VMEM] + [ANY] * 6,
        at, own, pt.reshape(2 * rows, tests), *crossed[0], *crossed[1],
    )
    slots = lax.all_to_all(slots, ("z", "x"), split_axis=0, concat_axis=0, tiled=True)
    mirror = slots[:, 2 * rows :]
    mirror = jnp.concatenate([mirror[..., : 2 * rows], mirror[..., 2 * rows :]], axis=1)

    keep, give = kernel_call(
        scores_kernel,
        [shape((tokens, tests), f32)] * 2,
        [SMEM] + [VMEM] * 3,
        at, slots, picked, arrived,
        flops=8 * 16 * rows * tokens * tests,
    )
    scores = keep + send(give, flip("c"))

    mirror = mirror.reshape(16 * rows, 2 * rows).T
    held = lax.dynamic_slice_in_dim(mirror, c * rows, rows, 0)
    given = send(lax.dynamic_slice_in_dim(mirror, (1 - c) * rows, rows, 0), flip("c"))
    (own,) = kernel_call(
        join_kernel, [shape((rows, feats), f32)], [SMEM] + [VMEM] * 3, at, direct, held, given
    )

    cross = second_stage(cross, crossed, rows)
    ours, theirs = jnp.where(yl == h, own, cross), jnp.where(yl == h, cross, own)
    term = ours + send(theirs.astype(bf16), flip("yl")).astype(f32)
    covariance_out = 0.9 * covariance + term / (tokens * 64)
    return scores, covariance_out


def solution(mesh):
    grid = Mesh(mesh.devices.reshape(SIZES), AXES)
    return jax.shard_map(
        on_device,
        mesh=grid,
        in_specs=(P(DP, "yh"), P(DP, "yh"), P("yh", DP), P(DP, None)),
        out_specs=(P(DP, "yh"), P(DP, "yh")),
        check_vma=False,
    )
```

```python
import functools

import jax
import jax.numpy as jnp
import numpy as np
from jax import lax
from jax.experimental import pallas as pl
from jax.experimental.pallas import tpu as pltpu
from jax.sharding import Mesh
from jax.sharding import PartitionSpec as P

AXES = ("yl", "z", "x", "c", "yh")
SIZES = (2, 4, 4, 2, 2)
DP = ("yl", "z", "x", "c")
NT = (((1,), (1,)), ((), ()))
TN = (((0,), (0,)), ((), ()))
bf16, f32 = jnp.bfloat16, jnp.float32
VMEM = pl.BlockSpec(memory_space=pltpu.VMEM)
ANY = pl.BlockSpec(memory_space=pl.ANY)
SMEM = pl.BlockSpec(memory_space=pltpu.SMEM)


def send(value, move, only=None):
    pairs = []
    for i in range(int(np.prod(SIZES))):
        at = dict(zip(AXES, (int(v) for v in np.unravel_index(i, SIZES))))
        if only is None or only(at):
            to = {**at, **move(at)}
            pairs.append((i, int(np.ravel_multi_index([to[a] for a in AXES], SIZES))))
    return lax.ppermute(value, AXES, pairs)


def along(axis, k):
    return lambda at: {axis: (at[axis] + k) % 4}


def flip(*axes):
    return lambda at: {a: 1 - at[a] for a in axes}


def kernel_call(body, outs, specs, *args, flops=0):
    nbytes = sum(a.size * a.dtype.itemsize for a in args) + sum(o.size * o.dtype.itemsize for o in outs)
    return pl.pallas_call(
        body,
        out_shape=outs,
        in_specs=specs,
        out_specs=[VMEM] * len(outs),
        cost_estimate=pl.CostEstimate(flops=flops, bytes_accessed=nbytes, transcendentals=0),
    )(*args)


def slots_kernel(f_ref, t_ref, out_ref):
    wide = f_ref.shape[1] // 32
    for s in range(16):
        out_ref[s, :, :wide] = f_ref[:, s * wide : (s + 1) * wide]
        out_ref[s, :, wide : 2 * wide] = f_ref[:, (16 + s) * wide : (17 + s) * wide]
        out_ref[s, :, 2 * wide :] = t_ref[...]


def factor_kernel(wide, slots_ref, after_ref, also_ref, out_ref):
    out_ref[...] = lax.dot_general(
        slots_ref[:, :wide], slots_ref[:, wide:], TN, preferred_element_type=f32
    )


def pick_kernel(at_ref, gt_ref, sib_ref, out_ref):
    for i, ref in enumerate((gt_ref, sib_ref)):
        for b in range(16):
            start = pl.ds(pl.multiple_of(b * 128 + at_ref[2], 64), 64)
            out_ref[(16 * i + b) * 64 : (16 * i + b + 1) * 64, :] = ref[start, :]


def own_kernel(a_ref, b1_ref, b2_ref, out_ref):
    rows = out_ref.shape[1]
    wide = 2 * rows
    for g in range(4):
        left1 = a_ref[4 * g * rows : 4 * (g + 1) * rows, :]
        left2 = a_ref[(16 + 4 * g) * rows : (20 + 4 * g) * rows, :]
        for q in range(3):
            cols = pl.ds((g + q) % 4 * 4 * wide, 4 * wide)
            acc = lax.dot_general(left1, b1_ref[cols, :], NT, preferred_element_type=f32)
            acc += lax.dot_general(left2, b2_ref[cols, :], NT, preferred_element_type=f32)
            acc = acc.astype(bf16)
            for i in range(4):
                lo, hi = max(4 * q, i), min(4 * q + 4, i + 9)
                if lo < hi:
                    piece = acc[i * rows : (i + 1) * rows, (lo - 4 * q) * wide : (hi - 4 * q) * wide]
                    out_ref[4 * g + i, :, (lo - i) * wide : (hi - i) * wide] = piece


def gram_kernel(at_ref, a_ref, b1_ref, b2_ref, after_ref, *outs):
    z, x = at_ref[0], at_ref[1]
    rows, m, n, tile = 64, a_ref.shape[0] // 2, b1_ref.shape[0] // 2, 256
    for half in range(2):
        left1, left2 = [], []
        for k in range(4):
            for j in range(4):
                dx, dz = (k, j) if half == 0 else (j, k)
                block = (lax.rem(z + dz, 4) * 4 + lax.rem(x + dx, 4)) * rows
                left1.append(a_ref[pl.ds(pl.multiple_of(block, rows), rows), :])
                left2.append(a_ref[pl.ds(pl.multiple_of(block + m, rows), rows), :])
        left1, left2 = jnp.concatenate(left1), jnp.concatenate(left2)
        for t in range(n // tile):
            cols = pl.ds(half * n + t * tile, tile)
            acc = lax.dot_general(left1, b1_ref[cols, :], NT, preferred_element_type=f32)
            acc += lax.dot_general(left2, b2_ref[cols, :], NT, preferred_element_type=f32)
            for k in range(4):
                part = acc[4 * k * rows : 4 * (k + 1) * rows].astype(bf16)
                outs[4 * half + k][:, t * tile : (t + 1) * tile] = part


def gram(at, a, b1, b2, after):
    n = b1.shape[0]
    return kernel_call(
        gram_kernel,
        [jax.ShapeDtypeStruct((256, n // 2), bf16)] * 8,
        [SMEM] + [VMEM] * 3 + [ANY],
        at, a, b1, b2, after,
        flops=2 * a.shape[0] * n * b1.shape[1],
    )


def scores_kernel(at_ref, pt_ref, own_ref, cross_ref, keep_ref, give_ref):
    h = at_ref[3]
    m = own_ref.shape[0] // 2
    p_own = pt_ref[:, pl.ds(pl.multiple_of(h * 64, 64), 64), :].reshape(m, pt_ref.shape[-1])
    p_cross = pt_ref[:, pl.ds(pl.multiple_of((1 - h) * 64, 64), 64), :].reshape(m, pt_ref.shape[-1])
    for side, out_ref in enumerate((keep_ref, give_ref)):
        s = slice(side * m, (side + 1) * m)
        acc = lax.dot_general(own_ref[s, :], p_own, TN, preferred_element_type=f32)
        out_ref[...] = acc + lax.dot_general(cross_ref[s, :], p_cross, TN, preferred_element_type=f32)


def first_stage(parts):
    got = []
    for half, axis in ((0, "x"), (1, "z")):
        got.append([send(parts[4 * half + k], along(axis, k)) for k in (1, 2, 3)])
    return got


def second_stage(parts, got, rows):
    sums = []
    for half, axis in ((0, "z"), (1, "x")):
        mids = []
        for j in range(4):
            cut = lambda v: lax.slice_in_dim(v, j * rows, (j + 1) * rows).astype(f32)
            total = cut(parts[4 * half])
            for r in got[half]:
                total = total + cut(r)
            mids.append(total)
        rs = [send(mids[k].astype(bf16), along(axis, k)) for k in (1, 2, 3)]
        sums.append(mids[0] + rs[0].astype(f32) + rs[1].astype(f32) + rs[2].astype(f32))
    return jnp.concatenate(sums, axis=1)


def own_sum_kernel(at_ref, got_ref, pt_ref, *refs):
    direct_ref, slots_ref = refs[-2:]
    chip = at_ref[0] * 4 + at_ref[1]
    rows = direct_ref.shape[0]
    wide, low = 2 * rows, rows // 2
    direct_ref[...] = jnp.zeros_like(direct_ref)
    slots_ref[:, :wide, :] = jnp.broadcast_to(pt_ref[...][None], (16, wide, pt_ref.shape[1]))
    slots_ref[:, wide:, :] = jnp.zeros_like(slots_ref[:, wide:, :])
    for k in range(9):
        total = jnp.sum(got_ref[:, :, k * wide : (k + 1) * wide].astype(f32), axis=0)
        to = lax.rem(chip + k, 16)
        direct_ref[:, pl.ds(pl.multiple_of(to * wide, wide), wide)] = total
        both = jnp.concatenate([total[:low], total[low:]], axis=1).astype(bf16)
        slots_ref[pl.ds(to, 1), wide:, :] = both[None]


def join_kernel(at_ref, direct_ref, held_ref, given_ref, out_ref):
    chip = at_ref[0] * 4 + at_ref[1]
    low = at_ref[2] == 0
    rows = held_ref.shape[0]
    for j in range(16):
        mine = held_ref[:, j * rows : (j + 1) * rows].astype(f32)
        other = given_ref[:, j * rows : (j + 1) * rows].astype(f32)
        both = jnp.concatenate([jnp.where(low, mine, other), jnp.where(low, other, mine)], axis=1)
        cols = slice(2 * j * rows, 2 * (j + 1) * rows)
        near = lax.rem(j - chip + 16, 16) <= 8
        out_ref[:, cols] = jnp.where(near, direct_ref[:, cols], both)


def on_device(grads, covariance, test_grads, inverse_factor):
    tokens, feats = grads.shape
    z, x, c = lax.axis_index("z"), lax.axis_index("x"), lax.axis_index("c")
    yl, h = lax.axis_index("yl"), lax.axis_index("yh")
    rows = feats // 32
    tests = test_grads.shape[0]
    at = jnp.stack([z, x, c * rows, h]).astype(jnp.int32)
    shape = jax.ShapeDtypeStruct
    gt = grads.T
    sib = send(gt, flip("c"))

    (picked,) = kernel_call(pick_kernel, [shape((feats, tokens), bf16)], [SMEM, VMEM, VMEM], at, gt, sib)
    arrived = send(picked, flip("yh"))
    (own,) = kernel_call(
        own_kernel,
        [shape((16, rows, 18 * rows), bf16)],
        [VMEM] * 3,
        picked, gt, sib,
        flops=3 * 16 * rows * feats * tokens,
    )

    (slots,) = kernel_call(
        slots_kernel,
        [shape((16, rows, 4 * rows + tests), bf16)],
        [VMEM, VMEM],
        inverse_factor, test_grads.T,
    )
    slots = lax.all_to_all(slots, ("z", "x"), split_axis=0, concat_axis=0, tiled=True)
    (pt,) = kernel_call(
        functools.partial(factor_kernel, 4 * rows),
        [shape((4 * rows, tests), f32)],
        [VMEM, ANY, ANY],
        slots.reshape(16 * rows, -1), own, picked,
        flops=2 * 16 * rows * 4 * rows * tests,
    )
    pt = pt.reshape(2, 2, rows, tests)
    half = lambda i: lax.dynamic_index_in_dim(pt, i, 1, keepdims=False)
    pt = half(c) + send(half(1 - c), flip("c"))
    pt = (pt + send(pt, flip("yl"))).astype(bf16)
    cross = gram(at, arrived, gt, sib, pt)
    crossed = first_stage(cross)

    own = lax.all_to_all(own, ("z", "x"), split_axis=0, concat_axis=0, tiled=True)
    direct, slots = kernel_call(
        own_sum_kernel,
        [shape((rows, feats), f32), shape((16, 2 * rows + rows // 2, tests), bf16)],
        [SMEM, VMEM, VMEM] + [ANY] * 6,
        at, own, pt.reshape(2 * rows, tests), *crossed[0], *crossed[1],
    )
    slots = lax.all_to_all(slots, ("z", "x"), split_axis=0, concat_axis=0, tiled=True)
    mirror = slots[:, 2 * rows :]
    mirror = jnp.concatenate([mirror[..., : 2 * rows], mirror[..., 2 * rows :]], axis=1)

    keep, give = kernel_call(
        scores_kernel,
        [shape((tokens, tests), f32)] * 2,
        [SMEM] + [VMEM] * 3,
        at, slots, picked, arrived,
        flops=8 * 16 * rows * tokens * tests,
    )
    scores = keep + send(give, flip("c"))

    mirror = mirror.reshape(16 * rows, 2 * rows).T
    held = lax.dynamic_slice_in_dim(mirror, c * rows, rows, 0)
    given = send(lax.dynamic_slice_in_dim(mirror, (1 - c) * rows, rows, 0), flip("c"))
    (own,) = kernel_call(
        join_kernel, [shape((rows, feats), f32)], [SMEM] + [VMEM] * 3, at, direct, held, given
    )

    cross = second_stage(cross, crossed, rows)
    ours, theirs = jnp.where(yl == h, own, cross), jnp.where(yl == h, cross, own)
    term = ours + send(theirs.astype(bf16), flip("yl")).astype(f32)
    covariance_out = 0.9 * covariance + term / (tokens * 64)
    return scores, covariance_out


def solution(mesh):
    grid = Mesh(mesh.devices.reshape(SIZES), AXES)
    return jax.shard_map(
        on_device,
        mesh=grid,
        in_specs=(P(DP, "yh"), P(DP, "yh"), P("yh", DP), P(DP, None)),
        out_specs=(P(DP, "yh"), P(DP, "yh")),
        check_vma=False,
    )
```

```python
import functools

import jax
import jax.numpy as jnp
import numpy as np
from jax import lax
from jax.experimental import pallas as pl
from jax.experimental.pallas import tpu as pltpu
from jax.sharding import Mesh
from jax.sharding import PartitionSpec as P

AXES = ("yl", "z", "x", "c", "yh")
SIZES = (2, 4, 4, 2, 2)
DP = ("yl", "z", "x", "c")
NT = (((1,), (1,)), ((), ()))
TN = (((0,), (0,)), ((), ()))
bf16, f32 = jnp.bfloat16, jnp.float32
VMEM = pl.BlockSpec(memory_space=pltpu.VMEM)
ANY = pl.BlockSpec(memory_space=pl.ANY)
SMEM = pl.BlockSpec(memory_space=pltpu.SMEM)


def send(value, move, only=None):
    pairs = []
    for i in range(int(np.prod(SIZES))):
        at = dict(zip(AXES, (int(v) for v in np.unravel_index(i, SIZES))))
        if only is None or only(at):
            to = {**at, **move(at)}
            pairs.append((i, int(np.ravel_multi_index([to[a] for a in AXES], SIZES))))
    return lax.ppermute(value, AXES, pairs)


def along(axis, k):
    return lambda at: {axis: (at[axis] + k) % 4}


def flip(*axes):
    return lambda at: {a: 1 - at[a] for a in axes}


def kernel_call(body, outs, specs, *args, flops=0):
    nbytes = sum(a.size * a.dtype.itemsize for a in args) + sum(o.size * o.dtype.itemsize for o in outs)
    return pl.pallas_call(
        body,
        out_shape=outs,
        in_specs=specs,
        out_specs=[VMEM] * len(outs),
        cost_estimate=pl.CostEstimate(flops=flops, bytes_accessed=nbytes, transcendentals=0),
    )(*args)


def slots_kernel(f_ref, t_ref, out_ref):
    wide = f_ref.shape[1] // 32
    for s in range(16):
        out_ref[s, :, :wide] = f_ref[:, s * wide : (s + 1) * wide]
        out_ref[s, :, wide : 2 * wide] = f_ref[:, (16 + s) * wide : (17 + s) * wide]
        out_ref[s, :, 2 * wide :] = t_ref[...]


def factor_kernel(wide, slots_ref, after_ref, also_ref, out_ref):
    out_ref[...] = lax.dot_general(
        slots_ref[:, :wide], slots_ref[:, wide:], TN, preferred_element_type=f32
    )


def own_kernel(a1_ref, a2_ref, b1_ref, b2_ref, out_ref):
    rows = out_ref.shape[1]
    wide = 2 * rows
    for g in range(4):
        left1 = a1_ref[4 * g * rows : 4 * (g + 1) * rows, :]
        left2 = a2_ref[4 * g * rows : 4 * (g + 1) * rows, :]
        for q in range(3):
            cols = pl.ds((g + q) % 4 * 4 * wide, 4 * wide)
            acc = lax.dot_general(left1, b1_ref[cols, :], NT, preferred_element_type=f32)
            acc += lax.dot_general(left2, b2_ref[cols, :], NT, preferred_element_type=f32)
            acc = acc.astype(bf16)
            for i in range(4):
                lo, hi = max(4 * q, i), min(4 * q + 4, i + 9)
                if lo < hi:
                    piece = acc[i * rows : (i + 1) * rows, (lo - 4 * q) * wide : (hi - 4 * q) * wide]
                    out_ref[4 * g + i, :, (lo - i) * wide : (hi - i) * wide] = piece


def gram_kernel(at_ref, a1_ref, a2_ref, b1_ref, b2_ref, after_ref, *outs):
    z, x = at_ref[0], at_ref[1]
    rows, n, tile = 64, b1_ref.shape[0] // 2, 256
    for half in range(2):
        left1, left2 = [], []
        for k in range(4):
            for j in range(4):
                dx, dz = (k, j) if half == 0 else (j, k)
                block = (lax.rem(z + dz, 4) * 4 + lax.rem(x + dx, 4)) * rows
                left1.append(a1_ref[pl.ds(pl.multiple_of(block, rows), rows), :])
                left2.append(a2_ref[pl.ds(pl.multiple_of(block, rows), rows), :])
        left1, left2 = jnp.concatenate(left1), jnp.concatenate(left2)
        for t in range(n // tile):
            cols = pl.ds(half * n + t * tile, tile)
            acc = lax.dot_general(left1, b1_ref[cols, :], NT, preferred_element_type=f32)
            acc += lax.dot_general(left2, b2_ref[cols, :], NT, preferred_element_type=f32)
            for k in range(4):
                part = acc[4 * k * rows : 4 * (k + 1) * rows].astype(bf16)
                outs[4 * half + k][:, t * tile : (t + 1) * tile] = part


def gram(at, a1, a2, b1, b2, after):
    n = b1.shape[0]
    return kernel_call(
        gram_kernel,
        [jax.ShapeDtypeStruct((256, n // 2), bf16)] * 8,
        [SMEM] + [VMEM] * 4 + [ANY],
        at, a1, a2, b1, b2, after,
        flops=4 * a1.shape[0] * n * b1.shape[1],
    )


def scores_kernel(at_ref, pt_ref, own1_ref, own2_ref, cross1_ref, cross2_ref, keep_ref, give_ref):
    h = at_ref[3]
    m = own1_ref.shape[0]
    p_own = pt_ref[:, pl.ds(pl.multiple_of(h * 64, 64), 64), :].reshape(m, pt_ref.shape[-1])
    p_cross = pt_ref[:, pl.ds(pl.multiple_of((1 - h) * 64, 64), 64), :].reshape(m, pt_ref.shape[-1])
    for own, cross, out_ref in ((own1_ref, cross1_ref, keep_ref), (own2_ref, cross2_ref, give_ref)):
        acc = lax.dot_general(own[...], p_own, TN, preferred_element_type=f32)
        out_ref[...] = acc + lax.dot_general(cross[...], p_cross, TN, preferred_element_type=f32)


def first_stage(parts):
    got = []
    for half, axis in ((0, "x"), (1, "z")):
        got.append([send(parts[4 * half + k], along(axis, k)) for k in (1, 2, 3)])
    return got


def second_stage(parts, got, rows):
    sums = []
    for half, axis in ((0, "z"), (1, "x")):
        mids = []
        for j in range(4):
            cut = lambda v: lax.slice_in_dim(v, j * rows, (j + 1) * rows).astype(f32)
            total = cut(parts[4 * half])
            for r in got[half]:
                total = total + cut(r)
            mids.append(total)
        rs = [send(mids[k].astype(bf16), along(axis, k)) for k in (1, 2, 3)]
        sums.append(mids[0] + rs[0].astype(f32) + rs[1].astype(f32) + rs[2].astype(f32))
    return jnp.concatenate(sums, axis=1)


def own_sum_kernel(at_ref, got_ref, pt_ref, *refs):
    direct_ref, slots_ref = refs[-2:]
    chip = at_ref[0] * 4 + at_ref[1]
    rows = direct_ref.shape[0]
    wide, low = 2 * rows, rows // 2
    direct_ref[...] = jnp.zeros_like(direct_ref)
    slots_ref[:, :wide, :] = jnp.broadcast_to(pt_ref[...][None], (16, wide, pt_ref.shape[1]))
    slots_ref[:, wide:, :] = jnp.zeros_like(slots_ref[:, wide:, :])
    for k in range(9):
        total = jnp.sum(got_ref[:, :, k * wide : (k + 1) * wide].astype(f32), axis=0)
        to = lax.rem(chip + k, 16)
        direct_ref[:, pl.ds(pl.multiple_of(to * wide, wide), wide)] = total
        both = jnp.concatenate([total[:low], total[low:]], axis=1).astype(bf16)
        slots_ref[pl.ds(to, 1), wide:, :] = both[None]


def join_kernel(at_ref, direct_ref, held_ref, given_ref, out_ref):
    chip = at_ref[0] * 4 + at_ref[1]
    low = at_ref[2] == 0
    rows = held_ref.shape[0]
    for j in range(16):
        mine = held_ref[:, j * rows : (j + 1) * rows].astype(f32)
        other = given_ref[:, j * rows : (j + 1) * rows].astype(f32)
        both = jnp.concatenate([jnp.where(low, mine, other), jnp.where(low, other, mine)], axis=1)
        cols = slice(2 * j * rows, 2 * (j + 1) * rows)
        near = lax.rem(j - chip + 16, 16) <= 8
        out_ref[:, cols] = jnp.where(near, direct_ref[:, cols], both)


def on_device(grads, covariance, test_grads, inverse_factor):
    tokens, feats = grads.shape
    z, x, c = lax.axis_index("z"), lax.axis_index("x"), lax.axis_index("c")
    yl, h = lax.axis_index("yl"), lax.axis_index("yh")
    rows = feats // 32
    tests = test_grads.shape[0]
    at = jnp.stack([z, x, c * rows, h]).astype(jnp.int32)
    shape = jax.ShapeDtypeStruct
    gt = grads.T
    sib = send(gt, flip("c"))

    pick = lambda v: lax.dynamic_index_in_dim(v.reshape(16, 2, rows, tokens), c, 1, keepdims=False)
    mine = pick(gt).reshape(feats // 2, tokens)
    far1 = send(mine, flip("yh"))
    sib_mine = pick(sib).reshape(feats // 2, tokens)
    far2 = send(sib_mine, flip("yh"))
    (own,) = kernel_call(
        own_kernel,
        [shape((16, rows, 18 * rows), bf16)],
        [VMEM] * 4,
        mine, sib_mine, gt, sib,
        flops=3 * 16 * rows * feats * tokens,
    )

    (slots,) = kernel_call(
        slots_kernel,
        [shape((16, rows, 4 * rows + tests), bf16)],
        [VMEM, VMEM],
        inverse_factor, test_grads.T,
    )
    slots = lax.all_to_all(slots, ("z", "x"), split_axis=0, concat_axis=0, tiled=True)
    (pt,) = kernel_call(
        functools.partial(factor_kernel, 4 * rows),
        [shape((4 * rows, tests), f32)],
        [VMEM, ANY, ANY],
        slots.reshape(16 * rows, -1), own, mine,
        flops=2 * 16 * rows * 4 * rows * tests,
    )
    pt = pt.reshape(2, 2, rows, tests)
    half = lambda i: lax.dynamic_index_in_dim(pt, i, 1, keepdims=False)
    pt = half(c) + send(half(1 - c), flip("c"))
    pt = (pt + send(pt, flip("yl"))).astype(bf16)
    cross = gram(at, far1, far2, gt, sib, pt)
    crossed = first_stage(cross)

    own = lax.all_to_all(own, ("z", "x"), split_axis=0, concat_axis=0, tiled=True)
    direct, slots = kernel_call(
        own_sum_kernel,
        [shape((rows, feats), f32), shape((16, 2 * rows + rows // 2, tests), bf16)],
        [SMEM, VMEM, VMEM] + [ANY] * 6,
        at, own, pt.reshape(2 * rows, tests), *crossed[0], *crossed[1],
    )
    slots = lax.all_to_all(slots, ("z", "x"), split_axis=0, concat_axis=0, tiled=True)
    mirror = slots[:, 2 * rows :]
    mirror = jnp.concatenate([mirror[..., : 2 * rows], mirror[..., 2 * rows :]], axis=1)

    keep, give = kernel_call(
        scores_kernel,
        [shape((tokens, tests), f32)] * 2,
        [SMEM] + [VMEM] * 5,
        at, slots, mine, sib_mine, far1, far2,
        flops=8 * 16 * rows * tokens * tests,
    )
    scores = keep + send(give, flip("c"))

    mirror = mirror.reshape(16 * rows, 2 * rows).T
    held = lax.dynamic_slice_in_dim(mirror, c * rows, rows, 0)
    given = send(lax.dynamic_slice_in_dim(mirror, (1 - c) * rows, rows, 0), flip("c"))
    (own,) = kernel_call(
        join_kernel, [shape((rows, feats), f32)], [SMEM] + [VMEM] * 3, at, direct, held, given
    )

    cross = second_stage(cross, crossed, rows)
    ours, theirs = jnp.where(yl == h, own, cross), jnp.where(yl == h, cross, own)
    term = ours + send(theirs.astype(bf16), flip("yl")).astype(f32)
    covariance_out = 0.9 * covariance + term / (tokens * 64)
    return scores, covariance_out


def solution(mesh):
    grid = Mesh(mesh.devices.reshape(SIZES), AXES)
    return jax.shard_map(
        on_device,
        mesh=grid,
        in_specs=(P(DP, "yh"), P(DP, "yh"), P("yh", DP), P(DP, None)),
        out_specs=(P(DP, "yh"), P(DP, "yh")),
        check_vma=False,
    )
```

```python
import functools

import jax
import jax.numpy as jnp
import numpy as np
from jax import lax
from jax.experimental import pallas as pl
from jax.experimental.pallas import tpu as pltpu
from jax.sharding import Mesh
from jax.sharding import PartitionSpec as P

AXES = ("yl", "z", "x", "c", "yh")
SIZES = (2, 4, 4, 2, 2)
DP = ("yl", "z", "x", "c")
NT = (((1,), (1,)), ((), ()))
TN = (((0,), (0,)), ((), ()))
bf16, f32 = jnp.bfloat16, jnp.float32
VMEM = pl.BlockSpec(memory_space=pltpu.VMEM)
ANY = pl.BlockSpec(memory_space=pl.ANY)
SMEM = pl.BlockSpec(memory_space=pltpu.SMEM)


def send(value, move, only=None):
    pairs = []
    for i in range(int(np.prod(SIZES))):
        at = dict(zip(AXES, (int(v) for v in np.unravel_index(i, SIZES))))
        if only is None or only(at):
            to = {**at, **move(at)}
            pairs.append((i, int(np.ravel_multi_index([to[a] for a in AXES], SIZES))))
    return lax.ppermute(value, AXES, pairs)


def along(axis, k):
    return lambda at: {axis: (at[axis] + k) % 4}


def flip(*axes):
    return lambda at: {a: 1 - at[a] for a in axes}


def kernel_call(body, outs, specs, *args, flops=0):
    nbytes = sum(a.size * a.dtype.itemsize for a in args) + sum(o.size * o.dtype.itemsize for o in outs)
    return pl.pallas_call(
        body,
        out_shape=outs,
        in_specs=specs,
        out_specs=[VMEM] * len(outs),
        cost_estimate=pl.CostEstimate(flops=flops, bytes_accessed=nbytes, transcendentals=0),
    )(*args)


def slots_kernel(f_ref, t_ref, out_ref):
    wide = f_ref.shape[1] // 32
    for s in range(16):
        out_ref[s, :, :wide] = f_ref[:, s * wide : (s + 1) * wide]
        out_ref[s, :, wide : 2 * wide] = f_ref[:, (16 + s) * wide : (17 + s) * wide]
        out_ref[s, :, 2 * wide :] = t_ref[...]


def factor_kernel(wide, slots_ref, after_ref, also_ref, out_ref):
    out_ref[...] = lax.dot_general(
        slots_ref[:, :wide], slots_ref[:, wide:], TN, preferred_element_type=f32
    )


def own_kernel(a1_ref, a2_ref, b1_ref, b2_ref, out_ref):
    rows = out_ref.shape[1]
    wide = 2 * rows
    for g in range(4):
        left1 = a1_ref[4 * g * rows : 4 * (g + 1) * rows, :]
        left2 = a2_ref[4 * g * rows : 4 * (g + 1) * rows, :]
        for q in range(3):
            cols = pl.ds((g + q) % 4 * 4 * wide, 4 * wide)
            acc = lax.dot_general(left1, b1_ref[cols, :], NT, preferred_element_type=f32)
            acc += lax.dot_general(left2, b2_ref[cols, :], NT, preferred_element_type=f32)
            acc = acc.astype(bf16)
            for i in range(4):
                lo, hi = max(4 * q, i), min(4 * q + 4, i + 9)
                if lo < hi:
                    piece = acc[i * rows : (i + 1) * rows, (lo - 4 * q) * wide : (hi - 4 * q) * wide]
                    out_ref[4 * g + i, :, (lo - i) * wide : (hi - i) * wide] = piece


def gram_kernel(at_ref, a1_ref, a2_ref, b1_ref, b2_ref, after_ref, *outs):
    z, x = at_ref[0], at_ref[1]
    rows, n, tile = 64, b1_ref.shape[0] // 2, 256
    for half in range(2):
        left1, left2 = [], []
        for k in range(4):
            for j in range(4):
                dx, dz = (k, j) if half == 0 else (j, k)
                block = (lax.rem(z + dz, 4) * 4 + lax.rem(x + dx, 4)) * rows
                left1.append(a1_ref[pl.ds(pl.multiple_of(block, rows), rows), :])
                left2.append(a2_ref[pl.ds(pl.multiple_of(block, rows), rows), :])
        left1, left2 = jnp.concatenate(left1), jnp.concatenate(left2)
        for t in range(n // tile):
            cols = pl.ds(half * n + t * tile, tile)
            acc = lax.dot_general(left1, b1_ref[cols, :], NT, preferred_element_type=f32)
            acc += lax.dot_general(left2, b2_ref[cols, :], NT, preferred_element_type=f32)
            for k in range(4):
                part = acc[4 * k * rows : 4 * (k + 1) * rows].astype(bf16)
                outs[4 * half + k][:, t * tile : (t + 1) * tile] = part


def gram(at, a1, a2, b1, b2, after):
    n = b1.shape[0]
    return kernel_call(
        gram_kernel,
        [jax.ShapeDtypeStruct((256, n // 2), bf16)] * 8,
        [SMEM] + [VMEM] * 4 + [ANY],
        at, a1, a2, b1, b2, after,
        flops=4 * a1.shape[0] * n * b1.shape[1],
    )


def scores_kernel(at_ref, pt_ref, own1_ref, own2_ref, cross1_ref, cross2_ref, keep_ref, give_ref):
    h = at_ref[3]
    m = own1_ref.shape[0]
    p_own = pt_ref[:, pl.ds(pl.multiple_of(h * 64, 64), 64), :].reshape(m, pt_ref.shape[-1])
    p_cross = pt_ref[:, pl.ds(pl.multiple_of((1 - h) * 64, 64), 64), :].reshape(m, pt_ref.shape[-1])
    for own, cross, out_ref in ((own1_ref, cross1_ref, keep_ref), (own2_ref, cross2_ref, give_ref)):
        acc = lax.dot_general(own[...], p_own, TN, preferred_element_type=f32)
        out_ref[...] = acc + lax.dot_general(cross[...], p_cross, TN, preferred_element_type=f32)


def first_stage(parts):
    got = []
    for half, axis in ((0, "x"), (1, "z")):
        got.append([send(parts[4 * half + k], along(axis, k)) for k in (1, 2, 3)])
    return got


def second_stage(parts, got, rows):
    sums = []
    for half, axis in ((0, "z"), (1, "x")):
        mids = []
        for j in range(4):
            cut = lambda v: lax.slice_in_dim(v, j * rows, (j + 1) * rows).astype(f32)
            total = cut(parts[4 * half])
            for r in got[half]:
                total = total + cut(r)
            mids.append(total)
        rs = [send(mids[k].astype(bf16), along(axis, k)) for k in (1, 2, 3)]
        sums.append(mids[0] + rs[0].astype(f32) + rs[1].astype(f32) + rs[2].astype(f32))
    return jnp.concatenate(sums, axis=1)


def own_sum_kernel(at_ref, got_ref, pt_ref, *refs):
    direct_ref, slots_ref = refs[-2:]
    chip = at_ref[0] * 4 + at_ref[1]
    rows = direct_ref.shape[0]
    wide, low = 2 * rows, rows // 2
    direct_ref[...] = jnp.zeros_like(direct_ref)
    slots_ref[:, :wide, :] = jnp.broadcast_to(pt_ref[...][None], (16, wide, pt_ref.shape[1]))
    slots_ref[:, wide:, :] = jnp.zeros_like(slots_ref[:, wide:, :])
    for k in range(9):
        total = jnp.sum(got_ref[:, :, k * wide : (k + 1) * wide].astype(f32), axis=0)
        to = lax.rem(chip + k, 16)
        direct_ref[:, pl.ds(pl.multiple_of(to * wide, wide), wide)] = total
        both = jnp.concatenate([total[:low], total[low:]], axis=1).astype(bf16)
        slots_ref[pl.ds(to, 1), wide:, :] = both[None]


def join_kernel(at_ref, direct_ref, held_ref, given_ref, out_ref):
    chip = at_ref[0] * 4 + at_ref[1]
    low = at_ref[2] == 0
    rows = held_ref.shape[0]
    for j in range(16):
        mine = held_ref[:, j * rows : (j + 1) * rows].astype(f32)
        other = given_ref[:, j * rows : (j + 1) * rows].astype(f32)
        both = jnp.concatenate([jnp.where(low, mine, other), jnp.where(low, other, mine)], axis=1)
        cols = slice(2 * j * rows, 2 * (j + 1) * rows)
        near = lax.rem(j - chip + 16, 16) <= 8
        out_ref[:, cols] = jnp.where(near, direct_ref[:, cols], both)


def on_device(grads, covariance, test_grads, inverse_factor):
    tokens, feats = grads.shape
    z, x, c = lax.axis_index("z"), lax.axis_index("x"), lax.axis_index("c")
    yl, h = lax.axis_index("yl"), lax.axis_index("yh")
    rows = feats // 32
    tests = test_grads.shape[0]
    at = jnp.stack([z, x, c * rows, h]).astype(jnp.int32)
    shape = jax.ShapeDtypeStruct
    gt = grads.T
    sib = send(gt, flip("c"))

    pick = lambda v: lax.dynamic_index_in_dim(v.reshape(16, 2, rows, tokens), c, 1, keepdims=False)
    mine = pick(gt).reshape(feats // 2, tokens)
    far1 = send(mine, flip("yh"))
    sib_mine = pick(sib).reshape(feats // 2, tokens)
    far2 = send(sib_mine, flip("yh"))
    (own,) = kernel_call(
        own_kernel,
        [shape((16, rows, 18 * rows), bf16)],
        [VMEM] * 4,
        mine, sib_mine, gt, sib,
        flops=3 * 16 * rows * feats * tokens,
    )

    (slots,) = kernel_call(
        slots_kernel,
        [shape((16, rows, 4 * rows + tests), bf16)],
        [VMEM, VMEM],
        inverse_factor, test_grads.T,
    )
    slots = lax.all_to_all(slots, ("z", "x"), split_axis=0, concat_axis=0, tiled=True)
    (pt,) = kernel_call(
        functools.partial(factor_kernel, 4 * rows),
        [shape((4 * rows, tests), f32)],
        [VMEM, ANY, ANY],
        slots.reshape(16 * rows, -1), own, mine,
        flops=2 * 16 * rows * 4 * rows * tests,
    )
    pt = pt.reshape(2, 2, rows, tests)
    half = lambda i: lax.dynamic_index_in_dim(pt, i, 1, keepdims=False)
    pt = half(c) + send(half(1 - c), flip("c"))
    pt = (pt + send(pt, flip("yl"))).astype(bf16)
    cross = gram(at, far1, far2, gt, sib, pt)
    crossed = first_stage(cross)

    own = lax.all_to_all(own, ("z", "x"), split_axis=0, concat_axis=0, tiled=True)
    direct, slots = kernel_call(
        own_sum_kernel,
        [shape((rows, feats), f32), shape((16, 2 * rows + rows // 2, tests), bf16)],
        [SMEM, VMEM, VMEM] + [ANY] * 5,
        at, own, pt.reshape(2 * rows, tests), *crossed[0], *crossed[1][:2],
    )
    slots = lax.all_to_all(slots, ("z", "x"), split_axis=0, concat_axis=0, tiled=True)
    mirror = slots[:, 2 * rows :]
    mirror = jnp.concatenate([mirror[..., : 2 * rows], mirror[..., 2 * rows :]], axis=1)

    keep, give = kernel_call(
        scores_kernel,
        [shape((tokens, tests), f32)] * 2,
        [SMEM] + [VMEM] * 5,
        at, slots, mine, sib_mine, far1, far2,
        flops=8 * 16 * rows * tokens * tests,
    )
    scores = keep + send(give, flip("c"))

    mirror = mirror.reshape(16 * rows, 2 * rows).T
    held = lax.dynamic_slice_in_dim(mirror, c * rows, rows, 0)
    given = send(lax.dynamic_slice_in_dim(mirror, (1 - c) * rows, rows, 0), flip("c"))
    (own,) = kernel_call(
        join_kernel, [shape((rows, feats), f32)], [SMEM] + [VMEM] * 3, at, direct, held, given
    )

    cross = second_stage(cross, crossed, rows)
    ours, theirs = jnp.where(yl == h, own, cross), jnp.where(yl == h, cross, own)
    term = ours + send(theirs.astype(bf16), flip("yl")).astype(f32)
    covariance_out = 0.9 * covariance + term / (tokens * 64)
    return scores, covariance_out


def solution(mesh):
    grid = Mesh(mesh.devices.reshape(SIZES), AXES)
    return jax.shard_map(
        on_device,
        mesh=grid,
        in_specs=(P(DP, "yh"), P(DP, "yh"), P("yh", DP), P(DP, None)),
        out_specs=(P(DP, "yh"), P(DP, "yh")),
        check_vma=False,
    )
```
